32 devices in a mesh: dp: 16 (over z, x, core), tensor: 2 (over y).
Axes of the slice: x: 2, y: 2, z: 4, core: 2. Of those that a mesh axis runs over, the one named last changes fastest.
Arguments:
- patches: bfloat16 [96, 512, 768], P('dp'), may hold values from -6 to 6
- counts: int32 [96], P('dp'), may hold values from 51 to 256, as said below
- visible: int32 [96, 512], P('dp'), may hold values from 0 to 511, each once within a row
- gain_one: float32 [768], replicated, may hold values from 0.1 to 1.9
- shift_one: float32 [768], replicated, may hold values from -2 to 2
- qkv_weight: bfloat16 [768, 3, 768], P(None, None, 'tensor'), may hold values from -0.21875 to 0.21875
- out_weight: bfloat16 [768, 768], P('tensor'), may hold values from -2 to 2
- gain_two: float32 [768], replicated, may hold values from 0.1 to 1.9
- shift_two: float32 [768], replicated, may hold values from -2 to 2
- up_weight: bfloat16 [768, 3072], P(None, 'tensor'), may hold values from -0.21875 to 0.21875
- down_weight: bfloat16 [3072, 768], P('tensor'), may hold values from -0.109375 to 0.109375
- cotangent: bfloat16 [96, 512, 768], P('dp'), may hold values from -6 to 6
Outputs:
- output: bfloat16 [96, 512, 768], P('dp')
- input_grad: bfloat16 [96, 512, 768], P('dp')
- gain_one_grad: float32 [768], replicated
- shift_one_grad: float32 [768], replicated
- qkv_grad: float32 [768, 3, 768], P(None, None, 'tensor')
- out_grad: float32 [768, 768], P('tensor')
- gain_two_grad: float32 [768], replicated
- shift_two_grad: float32 [768], replicated
- up_grad: float32 [768, 3072], P(None, 'tensor')
- down_grad: float32 [3072, 768], P('tensor')
The draws below stay inside these ranges and needn't reach their ends.
Inputs may be any that keep to these rules, and one draw needn't show every extreme that they name: `counts`: every sample has between 51 and 256 visible patches; some sample has exactly 256 and some exactly 51. Each row orders the 512 patches of a sample, its visible patches in the first counts places.
All inputs are finite; a program needn't handle non-finite values.
Results may differ from the reference program's by a relative error of at most 0.013.
Values sent between devices are 32-bit elements; how exact they have to be, the bound alone decides.
No kernel may reach another device: no remote copies, remote signals or barrier semaphores. Data moves between devices by JAX's collectives and lax.ppermute only.
A program may use at most 192 MiB of HBM per device.

```python
from functools import partial
import jax
import jax.numpy as jnp
from jax import lax

D = 768
HEADS = 12
HD = 64
FF = 3072
L = 512
SAMPLES = 96
VIS_LO = 51
VIS_HI = 256


def draw_counts(key, part):
    base = jax.random.randint(jax.random.fold_in(key, 11), (SAMPLES,), VIS_LO, VIS_HI + 1)
    picks = jax.random.permutation(jax.random.fold_in(key, 12), SAMPLES)
    places = jnp.arange(SAMPLES)
    base = jnp.where(places == picks[0], VIS_HI, base)
    base = jnp.where(places == picks[1], VIS_LO, base)
    return base.astype(jnp.int32)


def levels(rng, extent, pieces, low, largest):
    def one(position, shards_of):
        draws = jax.random.uniform(jax.random.fold_in(jax.random.fold_in(rng, 6), position), (shards_of,), jnp.float32, low / len(pieces), largest / len(pieces))
        return jnp.repeat(jnp.exp(draws), extent[position] // shards_of).reshape((-1,) + (1,) * (len(extent) - position - 1))

    factor_of = one(*pieces[0])
    for cut in pieces[1:]:
        factor_of = factor_of * one(*cut)
    return factor_of


def noise(rng, shape, scale, reach, cuts=(), dtype=jnp.bfloat16):
    values = scale * jax.random.normal(rng, shape, jnp.float32)
    if cuts:
        values = values * levels(rng, shape, cuts, -0.22, 0.18)
    return jnp.clip(values, -reach, reach).astype(dtype)


def setup_inputs(seed: int = 0) -> dict:
    keys = jax.random.split(jax.random.key(seed), 13)
    patches = noise(keys[0], (SAMPLES, L, D), 1.0, 6.0, ((0, 16),))
    counts = draw_counts(jax.random.fold_in(keys[12], 71), 0)
    visible = jax.vmap(lambda own: jax.random.permutation(own, L))(jax.random.split(keys[2], SAMPLES)).reshape((SAMPLES, L)).astype(jnp.int32)
    gain_one = jnp.clip(1.0 + 0.18 * jax.random.normal(keys[3], (D,), jnp.float32), 0.1, 1.9)
    shift_one = noise(keys[4], (D,), 0.4, 2.0, (), jnp.float32)
    qkv_weight = noise(keys[5], (D, 3, D), D ** -0.5, 0.21875, ((2, 2),))
    out_weight = noise(keys[6], (D, D), (max(1, D // 96)) ** -0.5, 2.0, ((0, 2),))
    gain_two = jnp.clip(1.0 + 0.18 * jax.random.normal(keys[7], (D,), jnp.float32), 0.1, 1.9)
    shift_two = noise(keys[8], (D,), 0.4, 2.0, (), jnp.float32)
    up_weight = noise(keys[9], (D, FF), D ** -0.5, 0.21875, ((1, 2),))
    down_weight = noise(keys[10], (FF, D), FF ** -0.5, 0.109375, ((0, 2),))
    cotangent = noise(keys[11], (SAMPLES, L, D), 1.0, 6.0, ((0, 16),))
    return {"patches": patches, "counts": counts, "visible": visible, "gain_one": gain_one, "shift_one": shift_one, "qkv_weight": qkv_weight, "out_weight": out_weight, "gain_two": gain_two, "shift_two": shift_two, "up_weight": up_weight, "down_weight": down_weight, "cotangent": cotangent}


@jax.custom_vjp
def low(v):
    return lax.optimization_barrier(v.astype(jnp.bfloat16)).astype(jnp.float32)

@jax.custom_vjp
def low_back(v):
    return v

def low_keep(v):
    return (low(v), None)

def low_pass(kept, grad):
    return (grad,)

def back_keep(v):
    return (v, None)

def back_low(kept, grad):
    return (low(grad),)
low.defvjp(low_keep, low_pass)
low_back.defvjp(back_keep, back_low)
norm_eps = 1e-06
masked_score = -1e+30
highest = lax.Precision.HIGHEST

def layer_norm(values, norm_gain, norm_shift):
    center = values - lax.optimization_barrier(jnp.mean(values, axis=-1, keepdims=True))
    spread = lax.optimization_barrier(jnp.mean(center * center, axis=-1, keepdims=True))
    return center * lax.rsqrt(spread + norm_eps) * norm_gain + norm_shift

def attend(block_items):
    query_rows, key_rows, value_rows, live_keys = block_items
    scores = jnp.einsum('qhd,khd->hqk', query_rows, key_rows, precision=highest) * HD ** (-0.5)
    scores = low_back(scores)
    scores = jnp.where(live_keys[None, None, :] > 0, scores, masked_score)
    row_max = lax.optimization_barrier(jnp.max(scores, axis=-1, keepdims=True))
    weights = jnp.exp(scores - row_max)
    probabilities = low(weights / lax.optimization_barrier(jnp.sum(weights, axis=-1, keepdims=True)))
    return jnp.einsum('hqk,khd->qhd', probabilities, value_rows, precision=highest)

def forward(patches, gain_one, shift_one, qkv_weight, out_weight, gain_two, shift_two, up_weight, down_weight, picked, live_mask, slot, grid_live):
    samples, slots, model_width = (patches.shape[0], picked.shape[1], patches.shape[2])
    row_count = samples * slots
    packed = jnp.take_along_axis(patches, picked[:, :, None], axis=1) * live_mask[:, :, None]
    resid_in = packed.reshape(row_count, model_width)
    normed_one = low(layer_norm(resid_in, gain_one, shift_one))
    projected = jnp.dot(normed_one, qkv_weight.reshape(model_width, 3 * model_width), precision=highest)
    projected = low(low_back(projected)).reshape(samples, slots, 3, HEADS, HD)
    attended = lax.map(jax.checkpoint(attend), (projected[:, :, 0], projected[:, :, 1], projected[:, :, 2], live_mask))
    attended = low(low_back(attended.reshape(row_count, model_width)))
    attn_out = low_back(jnp.dot(attended, out_weight, precision=highest))
    resid_mid = resid_in + attn_out
    normed_two = low(layer_norm(resid_mid, gain_two, shift_two))
    pre_act = low_back(jnp.dot(normed_two, up_weight, precision=highest))
    activation = low(jax.nn.gelu(pre_act, approximate=False))
    mlp_out = low_back(jnp.dot(activation, down_weight, precision=highest))
    result = (resid_mid + mlp_out).reshape(samples, slots, model_width) * live_mask[:, :, None]
    return jnp.take_along_axis(result, slot[:, :, None], axis=1) * grid_live[:, :, None]

def reference(patches, counts, visible, gain_one, shift_one, qkv_weight, out_weight, gain_two, shift_two, up_weight, down_weight, cotangent):
    picked = visible[:, :VIS_HI].astype(jnp.int32)
    live_mask = (lax.broadcasted_iota(jnp.int32, picked.shape, 1) < counts[:, None]).astype(jnp.float32)
    inverse = jnp.argsort(visible, axis=1).astype(jnp.int32)
    grid_live = (inverse < counts[:, None]).astype(jnp.float32)
    slot = jnp.minimum(inverse, VIS_HI - 1).astype(jnp.int32)
    inputs = (patches.astype(jnp.float32), gain_one, shift_one, qkv_weight.astype(jnp.float32), out_weight.astype(jnp.float32), gain_two, shift_two, up_weight.astype(jnp.float32), down_weight.astype(jnp.float32))
    layer = partial(forward, picked=picked, live_mask=live_mask, slot=slot, grid_live=grid_live)
    result, pullback = jax.vjp(layer, *inputs)
    gradients = pullback(cotangent.astype(jnp.float32))
    return (result.astype(jnp.bfloat16), gradients[0].astype(jnp.bfloat16), gradients[1], gradients[2], gradients[3], gradients[4], gradients[5], gradients[6], gradients[7], gradients[8])
```

```python
import jax
import jax.numpy as jnp
from jax import lax
from jax.sharding import Mesh, PartitionSpec as P
from jax.experimental import pallas as pl
from jax.experimental.pallas import tpu as pltpu

HD = 64
SLOTS = 256
TILE = 256
norm_eps = 1e-06
masked_score = -1e30
scale = HD ** (-0.5)
f32, bf16 = jnp.float32, jnp.bfloat16


def dot(x, y, dims=((1,), (0,))):
    return lax.dot_general(x, y, (dims, ((), ())), preferred_element_type=f32)


NT = ((1,), (1,))
TN = ((0,), (0,))


def rows_of(counts, samples):
    starts, total = [], 0
    for s in range(samples):
        starts.append(total)
        total = total + ((counts[s] + 15) // 16) * 16
    return starts, total


def win(start, size=SLOTS):
    if not isinstance(start, int):
        start = pl.multiple_of(start, 16)
    return pl.ds(start, size)


def start_of(counts, s):
    return lax.fori_loop(0, s, lambda i, t: t + ((counts[i] + 15) // 16) * 16, 0)


def total_of(counts, samples):
    return start_of(counts, samples)


def normed(values):
    center = values - jnp.mean(values, axis=-1, keepdims=True)
    spread = jnp.mean(center * center, axis=-1, keepdims=True)
    inv = lax.rsqrt(spread + norm_eps)
    return center * inv, inv


def norm_back(grad, hat, inv, gain):
    g = grad * gain
    return inv * (g - jnp.mean(g, axis=-1, keepdims=True) - hat * jnp.mean(g * hat, axis=-1, keepdims=True))


def lane_halves():
    lane = lax.broadcasted_iota(jnp.int32, (1, 128), 1)
    return lane < HD


def attend_rows(counts, qkv, out, lse, samples, width):
    left = lane_halves()
    row = lax.broadcasted_iota(jnp.int32, (SLOTS, 1), 0)

    def one(s, start):
        rows = win(start)
        live = row < counts[s]
        for pair in range(width // 128):
            lo = pair * 128
            q = qkv[rows, lo:lo + 128]
            k = qkv[rows, width + lo:width + lo + 128]
            v = qkv[rows, 2 * width + lo:2 * width + lo + 128]
            parts = []
            for side in range(2):
                keep = left if side == 0 else ~left
                sc = dot(jnp.where(keep, k, jnp.zeros_like(k)), q, NT) * scale
                sc = jnp.where(live, sc, masked_score)
                top = jnp.max(sc, axis=0, keepdims=True)
                w = jnp.exp(sc - top)
                tot = jnp.sum(w, axis=0, keepdims=True)
                lse[s, 2 * pair + side:2 * pair + side + 1, :] = top + jnp.log(tot)
                p = (w * (1.0 / tot)).astype(bf16)
                parts.append(dot(p, v, TN))
            out[rows, lo:lo + 128] = jnp.where(left, parts[0], parts[1]).astype(bf16)
        return start + ((counts[s] + 15) // 16) * 16

    lax.fori_loop(0, samples, one, 0)


def tiles(total):
    return (total + TILE - 1) // TILE


def fwd_own_body(samples, width):
    def body(counts, col, patches, cot, gain, shift, weight, h, dm, a, qkv, o, lse):
        s = pl.program_id(0)
        start = start_of(counts, s)
        pick = col[0, :SLOTS, :]
        row = lax.broadcasted_iota(jnp.int32, (SLOTS, 1), 0)
        pick = jnp.where(row < counts[s], pick, -1)
        hot = (lax.broadcasted_iota(jnp.int32, (SLOTS, patches.shape[1]), 1) == pick).astype(f32).astype(bf16)
        h[win(start), :] = dot(hot, patches[0]).astype(bf16)
        dm[win(start), :] = dot(hot, cot[0]).astype(bf16)

        @pl.when(s == samples - 1)
        def _():
            total = total_of(counts, samples)
            zeros = jnp.zeros((TILE, h.shape[1]), bf16)
            h[win(total), :] = zeros
            dm[win(total), :] = zeros

            def tile(i, c):
                r = win(i * TILE)
                hat, _ = normed(h[r, :].astype(f32))
                av = (hat * gain[...] + shift[...]).astype(bf16)
                a[r, :] = av
                qkv[r, :] = dot(av, weight[...]).astype(bf16)
                return c

            n = tiles(total)
            lax.fori_loop(0, n, tile, 0)
            qkv[win(n * TILE), :] = jnp.zeros((TILE, qkv.shape[1]), bf16)
            attend_rows(counts, qkv, o, lse, samples, width)
    return body


def fwd_other_body(samples, width):
    def body(counts, a, h, o, weight, out_own, out_other, gain, shift, qkv, o2, lse, r, c):
        total = total_of(counts, samples)
        n = tiles(total)

        def tile(i, x):
            rr = win(i * TILE)
            qkv[rr, :] = dot(a[rr, :], weight[...]).astype(bf16)
            return x

        lax.fori_loop(0, n, tile, 0)
        qkv[win(n * TILE), :] = jnp.zeros((TILE, qkv.shape[1]), bf16)
        attend_rows(counts, qkv, o2, lse, samples, width)

        def tail(i, x):
            rr = win(i * TILE)
            z = dot(o[rr, :], out_own[...]) + dot(o2[rr, :], out_other[...])
            rv = h[rr, :].astype(f32) + z
            r[rr, :] = rv
            hat, _ = normed(rv)
            c[rr, :] = (hat * gain[...] + shift[...]).astype(bf16)
            return x

        lax.fori_loop(0, n, tail, 0)
    return body


def gelu_both(u):
    cdf = 0.5 * (1.0 + lax.erf(u * (0.5 ** 0.5)))
    pdf = jnp.exp(-0.5 * u * u) * (0.5 / jnp.pi) ** 0.5
    return u * cdf, cdf + u * pdf


def mlp_tile(cv, dv, up, down):
    u = dot(cv, up[...])
    e, slope = gelu_both(u)
    e = e.astype(bf16)
    m = dot(e, down[...])
    de = dot(dv, down[...], NT)
    du = (de * slope).astype(bf16)
    dc = dot(du, up[...], NT)
    return e, du, m, dc


def mlp_own_body(samples):
    def body(counts, c, dm, up, down, m, dc, gup, gdown):
        n = tiles(total_of(counts, samples))
        gup[...] = jnp.zeros(gup.shape, f32)
        gdown[...] = jnp.zeros(gdown.shape, f32)

        def tile(i, x):
            r = win(i * TILE)
            cv, dv = c[r, :], dm[r, :]
            e, du, mv, dcv = mlp_tile(cv, dv, up, down)
            m[r, :] = mv
            dc[r, :] = dcv
            gdown[...] += dot(e, dv, TN)
            gup[...] += dot(cv, du, TN)
            return x

        lax.fori_loop(0, n, tile, 0)
    return body


def hot_back(counts, line, s, patches):
    live = lax.broadcasted_iota(jnp.int32, (1, SLOTS), 1) < counts[s]
    pick = jnp.where(live, line[s, :, :SLOTS], -1)
    return (lax.broadcasted_iota(jnp.int32, (patches, SLOTS), 0) == pick).astype(f32).astype(bf16)


def mlp_other_body(samples, patches):
    def body(counts, line, c, dm, up, down, m, dc, r, gain, out, dr, g2, y):
        n = tiles(total_of(counts, samples))
        g2[...] = jnp.zeros(g2.shape, f32)

        def tile(i, x):
            rr = win(i * TILE)
            cv, dv = c[rr, :], dm[rr, :]
            _, _, mv, dcv = mlp_tile(cv, dv, up, down)
            rv = r[rr, :]
            y[rr, :] = (rv + (m[rr, :] + mv)).astype(bf16)
            dct = dc[rr, :] + dcv
            hat, inv = normed(rv)
            g2[0:1, :] += jnp.sum(dct * hat, axis=0, keepdims=True)
            g2[1:2, :] += jnp.sum(dct, axis=0, keepdims=True)
            dr[rr, :] = dv.astype(f32) + norm_back(dct, hat, inv, gain[...])
            return x

        lax.fori_loop(0, n, tile, 0)
        y[win(n * TILE), :] = jnp.zeros((TILE, y.shape[1]), bf16)

        def scatter(s, start):
            out[s] = dot(hot_back(counts, line, s, patches), y[win(start), :]).astype(bf16)
            return start + ((counts[s] + 15) // 16) * 16

        lax.fori_loop(0, samples, scatter, 0)
    return body


def attend_back(counts, qkv, do, lse, dqkv, samples, width):
    left = lane_halves()
    row = lax.broadcasted_iota(jnp.int32, (SLOTS, 1), 0)

    def one(s, start):
        rows = win(start)
        live = row < counts[s]
        for pair in range(width // 128):
            lo = pair * 128
            q = qkv[rows, lo:lo + 128]
            k = qkv[rows, width + lo:width + lo + 128]
            v = qkv[rows, 2 * width + lo:2 * width + lo + 128]
            dov = do[rows, lo:lo + 128]
            dov = jnp.where(live, dov, jnp.zeros_like(dov))
            zero = jnp.zeros_like(k)
            dq, dk, dvv = [], [], []
            for side in range(2):
                keep = left if side == 0 else ~left
                sc = dot(jnp.where(keep, k, zero), q, NT) * scale
                sc = jnp.where(live, sc, masked_score)
                p = jnp.exp(sc - lse[s, 2 * pair + side:2 * pair + side + 1, :])
                dp = dot(jnp.where(keep, v, zero), dov, NT)
                t = jnp.sum(p * dp, axis=0, keepdims=True)
                ds = (p * (dp - t)).astype(bf16)
                dq.append(dot(ds, k, TN))
                dk.append(dot(ds, q))
                dvv.append(dot(p.astype(bf16), dov))
            dqkv[rows, lo:lo + 128] = (jnp.where(left, dq[0], dq[1]) * scale).astype(bf16)
            dqkv[rows, width + lo:width + lo + 128] = (jnp.where(left, dk[0], dk[1]) * scale).astype(bf16)
            dqkv[rows, 2 * width + lo:2 * width + lo + 128] = jnp.where(left, dvv[0], dvv[1]).astype(bf16)
        return start + ((counts[s] + 15) // 16) * 16

    lax.fori_loop(0, samples, one, 0)


def attn_own_body(samples, width):
    def body(counts, dr, qkv, lse, o, a, wout, wqkv, da, gout, gqkv, do, dqkv):
        total = total_of(counts, samples)
        n = tiles(total)
        gout[...] = jnp.zeros(gout.shape, f32)
        gqkv[...] = jnp.zeros(gqkv.shape, f32)

        def first(i, x):
            r = win(i * TILE)
            dz = dr[r, :].astype(bf16)
            do[r, :] = dot(dz, wout[...], NT).astype(bf16)
            gout[...] += dot(o[r, :], dz, TN)
            return x

        lax.fori_loop(0, n, first, 0)
        attend_back(counts, qkv, do, lse, dqkv, samples, width)
        dqkv[win(total), :] = jnp.zeros((TILE, dqkv.shape[1]), bf16)

        def last(i, x):
            r = win(i * TILE)
            dv = dqkv[r, :]
            da[r, :] = dot(dv, wqkv[...], NT)
            gqkv[...] += dot(a[r, :], dv, TN)
            return x

        lax.fori_loop(0, n, last, 0)
    return body


def attn_other_body(samples, width, patches):
    def body(counts, line, dr, qkv, lse, wout, wqkv, da, h, gain, out, g1, do, dqkv, dh):
        total = total_of(counts, samples)
        n = tiles(total)
        g1[...] = jnp.zeros(g1.shape, f32)

        def first(i, x):
            r = win(i * TILE)
            do[r, :] = dot(dr[r, :].astype(bf16), wout[...], NT).astype(bf16)
            return x

        lax.fori_loop(0, n, first, 0)
        attend_back(counts, qkv, do, lse, dqkv, samples, width)
        dqkv[win(total), :] = jnp.zeros((TILE, dqkv.shape[1]), bf16)

        def last(i, x):
            r = win(i * TILE)
            dat = da[r, :] + dot(dqkv[r, :], wqkv[...], NT)
            hat, inv = normed(h[r, :].astype(f32))
            g1[0:1, :] += jnp.sum(dat * hat, axis=0, keepdims=True)
            g1[1:2, :] += jnp.sum(dat, axis=0, keepdims=True)
            dh[r, :] = (dr[r, :] + norm_back(dat, hat, inv, gain[...])).astype(bf16)
            return x

        lax.fori_loop(0, n, last, 0)
        dh[win(n * TILE), :] = jnp.zeros((TILE, dh.shape[1]), bf16)

        def scatter(s, start):
            out[s] = dot(hot_back(counts, line, s, patches), dh[win(start), :]).astype(bf16)
            return start + ((counts[s] + 15) // 16) * 16

        lax.fori_loop(0, samples, scatter, 0)
    return body


def sds(shape, dtype):
    return jax.ShapeDtypeStruct(shape, dtype)


def call(body, name, counts, args, outs, scratch=(), flops=0):
    moved = sum(x.size * x.dtype.itemsize for x in list(args) + list(outs))
    return pl.pallas_call(
        body,
        name=name,
        out_shape=list(outs),
        grid_spec=pltpu.PrefetchScalarGridSpec(
            num_scalar_prefetch=1,
            grid=(1,),
            in_specs=[pl.BlockSpec(x.shape, lambda i, n, d=x.ndim: (0,) * d, pipeline_mode=pl.Buffered(1)) for x in args],
            out_specs=[pl.BlockSpec(x.shape, lambda i, n, d=len(x.shape): (0,) * d, pipeline_mode=pl.Buffered(1)) for x in outs],
            scratch_shapes=list(scratch),
        ),
        compiler_params=pltpu.CompilerParams(vmem_limit_bytes=62 << 20),
        cost_estimate=pl.CostEstimate(flops=flops, transcendentals=0, bytes_accessed=moved),
    )(counts, *args)


def fwd_own(counts, col, patches, cot, gain, shift, weight):
    S, L, D = patches.shape
    width = weight.shape[1] // 3
    TP = S * SLOTS + TILE
    whole = lambda d: (lambda s, n: (0,) * d)
    one = lambda s, n: (s, 0, 0)
    B1 = pl.Buffered(1)
    outs = [sds((TP, D), bf16), sds((TP, D), bf16), sds((TP, D), bf16), sds((TP, 3 * width), bf16), sds((TP, width), bf16), sds((S, width // HD, SLOTS), f32)]
    return pl.pallas_call(
        fwd_own_body(S, width),
        name="fwd_own",
        out_shape=outs,
        grid_spec=pltpu.PrefetchScalarGridSpec(
            num_scalar_prefetch=1,
            grid=(S,),
            in_specs=[
                pl.BlockSpec((1, L, 1), one),
                pl.BlockSpec((1, L, D), one),
                pl.BlockSpec((1, L, D), one),
                pl.BlockSpec((1, D), whole(2)),
                pl.BlockSpec((1, D), whole(2)),
                pl.BlockSpec(weight.shape, whole(2), pipeline_mode=B1),
            ],
            out_specs=[pl.BlockSpec(x.shape, whole(len(x.shape)), pipeline_mode=B1) for x in outs],
        ),
        compiler_params=pltpu.CompilerParams(vmem_limit_bytes=62 << 20),
        cost_estimate=pl.CostEstimate(flops=6 * 10**9, transcendentals=0, bytes_accessed=25 << 20),
    )(counts, col, patches, cot, gain, shift, weight)


def fwd_other(counts, a, h, o, weight, out_own, out_other, gain, shift, S):
    TP, D = a.shape
    width = weight.shape[1] // 3
    outs = [sds((TP, 3 * width), bf16), sds((TP, width), bf16), sds((S, width // HD, SLOTS), f32), sds((TP, D), f32), sds((TP, D), bf16)]
    return call(fwd_other_body(S, width), "fwd_other", counts, [a, h, o, weight, out_own, out_other, gain, shift], outs, flops=7 * 10**9)


def mlp_own(counts, c, dm, up, down, S):
    TP, D = c.shape
    outs = [sds((TP, D), f32), sds((TP, D), f32), sds(up.shape, f32), sds(down.shape, f32)]
    return call(mlp_own_body(S), "mlp_own", counts, [c, dm, up, down], outs, flops=18 * 10**9)


def mlp_other(counts, line, c, dm, up, down, m, dc, r, gain, S, L):
    TP, D = c.shape
    outs = [sds((S, L, D), bf16), sds((TP, D), f32), sds((8, D), f32)]
    return call(mlp_other_body(S, L), "mlp_other", counts, [line, c, dm, up, down, m, dc, r, gain], outs, [pltpu.VMEM((TP, D), bf16)], flops=12 * 10**9)


def attn_own(counts, dr, qkv, lse, o, a, wout, wqkv, S):
    TP, D = a.shape
    width = wout.shape[0]
    outs = [sds((TP, D), f32), sds(wout.shape, f32), sds(wqkv.shape, f32)]
    return call(attn_own_body(S, width), "attn_own", counts, [dr, qkv, lse, o, a, wout, wqkv], outs, [pltpu.VMEM((TP, width), bf16), pltpu.VMEM((TP, 3 * width), bf16)], flops=9 * 10**9)


def attn_other(counts, line, dr, qkv, lse, wout, wqkv, da, h, gain, S, L):
    TP, D = h.shape
    width = wout.shape[0]
    outs = [sds((S, L, D), bf16), sds((8, D), f32)]
    return call(attn_other_body(S, width, L), "attn_other", counts, [line, dr, qkv, lse, wout, wqkv, da, h, gain], outs, [pltpu.VMEM((TP, width), bf16), pltpu.VMEM((TP, 3 * width), bf16), pltpu.VMEM((TP, D), bf16)], flops=8 * 10**9)


def local(patches, counts, visible, g1, b1, g2, b2, cot, wq0, wo0, wu0, wd0, rest):
    S, L, D = patches.shape
    col, line = visible[:, :, None], visible[:, None, :]
    g1, b1, g2, b2 = (x[None, :] for x in (g1, b1, g2, b2))
    h, dm, a, qkv0, o0, lse0 = fwd_own(counts, col, patches, cot, g1, b1, wq0)
    wq1, wo1, wu1, wd1 = rest
    qkv1, o1, lse1, r, c = fwd_other(counts, a, h, o0, wq1, wo0, wo1, g2, b2, S)
    m, dc, gup, gdown = mlp_own(counts, c, dm, wu0, wd0, S)
    out, dr, gg2 = mlp_other(counts, line, c, dm, wu1, wd1, m, dc, r, g2, S, L)
    da, gout, gqkv = attn_own(counts, dr, qkv0, lse0, o0, a, wo0, wq0, S)
    gin, gg1 = attn_other(counts, line, dr, qkv1, lse1, wo1, wq1, da, h, g1, S, L)
    return out, gin, gg1, gqkv, gout, gg2, gup, gdown


def swap(x, axis, size, bit):
    return lax.ppermute(x, axis, [(k, k ^ bit) for k in range(size)])


def cast_pieces(order, pieces):
    rows, cols = pieces[0].shape

    def body(where, *refs):
        for i in range(4):
            refs[4][pl.ds(pl.multiple_of(where[i] * rows, 16), rows), :] = refs[i][...].astype(bf16)

    return call(body, "cast_pieces", order, pieces, [sds((4 * rows, cols), bf16)])[0]


def fetch(weight, dp):
    me = lax.axis_index("dp") % 4
    rows = weight.shape[0] // 4
    part = lax.dynamic_slice_in_dim(weight, me * rows, rows, 0).astype(f32)
    first = swap(part, "tensor", 2, 1)
    across = swap(first, "dp", dp, 2)
    order = jnp.stack([me, me ^ 2, me ^ 1, me ^ 3]).astype(jnp.int32)
    return cast_pieces(order, [first, across, swap(first, "dp", dp, 1), swap(across, "dp", dp, 1)])


def shards(dp, patches, counts, visible, g1, b1, wq, wo, g2, b2, wu, wd, cot):
    D = patches.shape[2]
    wq = wq.reshape(D, -1)
    rest = tuple(fetch(w, dp) for w in (wq, wo, wu, wd))
    out, gin, gg1, gqkv, gout, gg2, gup, gdown = local(patches, counts, visible, g1, b1, g2, b2, cot, wq, wo, wu, wd, rest)
    gup, gdown = lax.psum((gup, gdown), "dp")
    gqkv, gout, gg1, gg2 = lax.psum((gqkv, gout, gg1, gg2), "dp")
    return (out, gin, gg1[0], gg1[1], gqkv.reshape(D, 3, -1), gout, gg2[0], gg2[1], gup, gdown)


def solution(mesh):
    dp = mesh.shape["dp"]
    placed = (P("dp", None, None), P("dp"), P("dp", None), P(), P(), P(None, None, "tensor"), P("tensor", None), P(), P(), P(None, "tensor"), P("tensor", None), P("dp", None, None))
    outs = (P("dp", None, None), P("dp", None, None), P(), P(), P(None, None, "tensor"), P("tensor", None), P(), P(), P(None, "tensor"), P("tensor", None))
    return jax.shard_map(lambda *a: shards(dp, *a), mesh=mesh, in_specs=placed, out_specs=outs, check_vma=False)
```

```python
import jax
import jax.numpy as jnp
from jax import lax
from jax.sharding import Mesh, PartitionSpec as P
from jax.experimental import pallas as pl
from jax.experimental.pallas import tpu as pltpu

HD = 64
SLOTS = 256
TILE = 256
norm_eps = 1e-06
masked_score = -1e30
scale = HD ** (-0.5)
f32, bf16 = jnp.float32, jnp.bfloat16


def dot(x, y, dims=((1,), (0,))):
    return lax.dot_general(x, y, (dims, ((), ())), preferred_element_type=f32)


NT = ((1,), (1,))
TN = ((0,), (0,))


def rows_of(counts, samples):
    starts, total = [], 0
    for s in range(samples):
        starts.append(total)
        total = total + ((counts[s] + 15) // 16) * 16
    return starts, total


def win(start, size=SLOTS):
    if not isinstance(start, int):
        start = pl.multiple_of(start, 16)
    return pl.ds(start, size)


def start_of(counts, s):
    return lax.fori_loop(0, s, lambda i, t: t + ((counts[i] + 15) // 16) * 16, 0)


def total_of(counts, samples):
    return start_of(counts, samples)


def normed(values):
    center = values - jnp.mean(values, axis=-1, keepdims=True)
    spread = jnp.mean(center * center, axis=-1, keepdims=True)
    inv = lax.rsqrt(spread + norm_eps)
    return center * inv, inv


def norm_back(grad, hat, inv, gain):
    g = grad * gain
    return inv * (g - jnp.mean(g, axis=-1, keepdims=True) - hat * jnp.mean(g * hat, axis=-1, keepdims=True))


def lane_halves():
    lane = lax.broadcasted_iota(jnp.int32, (1, 128), 1)
    return lane < HD


def attend_rows(counts, qkv, out, lse, samples, width):
    left = lane_halves()
    row = lax.broadcasted_iota(jnp.int32, (SLOTS, 1), 0)

    def one(s, start):
        rows = win(start)
        live = row < counts[s]
        for pair in range(width // 128):
            lo = pair * 128
            q = qkv[rows, lo:lo + 128]
            k = qkv[rows, width + lo:width + lo + 128]
            v = qkv[rows, 2 * width + lo:2 * width + lo + 128]
            parts = []
            for side in range(2):
                keep = left if side == 0 else ~left
                sc = dot(jnp.where(keep, k, jnp.zeros_like(k)), q, NT) * scale
                sc = jnp.where(live, sc, masked_score)
                top = jnp.max(sc, axis=0, keepdims=True)
                w = jnp.exp(sc - top)
                tot = jnp.sum(w, axis=0, keepdims=True)
                lse[s, 2 * pair + side:2 * pair + side + 1, :] = top + jnp.log(tot)
                p = (w * (1.0 / tot)).astype(bf16)
                parts.append(dot(p, v, TN))
            out[rows, lo:lo + 128] = jnp.where(left, parts[0], parts[1]).astype(bf16)
        return start + ((counts[s] + 15) // 16) * 16

    lax.fori_loop(0, samples, one, 0)


def tiles(total):
    return (total + TILE - 1) // TILE


def fwd_own_body(samples, width):
    def body(counts, col, patches, cot, gain, shift, weight, h, dm, a, qkv, o, lse):
        s = pl.program_id(0)
        start = start_of(counts, s)
        pick = col[0, :SLOTS, :]
        row = lax.broadcasted_iota(jnp.int32, (SLOTS, 1), 0)
        pick = jnp.where(row < counts[s], pick, -1)
        hot = (lax.broadcasted_iota(jnp.int32, (SLOTS, patches.shape[1]), 1) == pick).astype(f32).astype(bf16)
        h[win(start), :] = dot(hot, patches[0]).astype(bf16)
        dm[win(start), :] = dot(hot, cot[0]).astype(bf16)

        @pl.when(s == samples - 1)
        def _():
            total = total_of(counts, samples)
            zeros = jnp.zeros((TILE, h.shape[1]), bf16)
            h[win(total), :] = zeros
            dm[win(total), :] = zeros

            def tile(i, c):
                r = win(i * TILE)
                hat, _ = normed(h[r, :].astype(f32))
                av = (hat * gain[...] + shift[...]).astype(bf16)
                a[r, :] = av
                qkv[r, :] = dot(av, weight[...]).astype(bf16)
                return c

            n = tiles(total)
            lax.fori_loop(0, n, tile, 0)
            qkv[win(n * TILE), :] = jnp.zeros((TILE, qkv.shape[1]), bf16)
            attend_rows(counts, qkv, o, lse, samples, width)
            o[win(total), :] = jnp.zeros((TILE, width), bf16)
    return body


def fwd_other_body(samples, width):
    def body(counts, a, h, o, weight, out_own, out_other, gain, shift, qkv, o2, lse, r, c):
        total = total_of(counts, samples)
        n = tiles(total)

        def tile(i, x):
            rr = win(i * TILE)
            qkv[rr, :] = dot(a[rr, :], weight[...]).astype(bf16)
            return x

        lax.fori_loop(0, n, tile, 0)
        qkv[win(n * TILE), :] = jnp.zeros((TILE, qkv.shape[1]), bf16)
        attend_rows(counts, qkv, o2, lse, samples, width)
        o2[win(total), :] = jnp.zeros((TILE, width), bf16)

        def tail(i, x):
            rr = win(i * TILE)
            z = dot(o[rr, :], out_own[...]) + dot(o2[rr, :], out_other[...])
            rv = h[rr, :].astype(f32) + z
            r[rr, :] = rv
            hat, _ = normed(rv)
            c[rr, :] = (hat * gain[...] + shift[...]).astype(bf16)
            return x

        lax.fori_loop(0, n, tail, 0)
    return body


def gelu_both(u):
    cdf = 0.5 * (1.0 + lax.erf(u * (0.5 ** 0.5)))
    pdf = jnp.exp(-0.5 * u * u) * (0.5 / jnp.pi) ** 0.5
    return u * cdf, cdf + u * pdf


def mlp_tile(cv, dv, up, down):
    u = dot(cv, up[...])
    e, slope = gelu_both(u)
    e = e.astype(bf16)
    m = dot(e, down[...])
    de = dot(dv, down[...], NT)
    du = (de * slope).astype(bf16)
    dc = dot(du, up[...], NT)
    return e, du, m, dc


def mlp_own_body(samples):
    def body(counts, c, dm, up, down, m, dc, gup, gdown):
        n = tiles(total_of(counts, samples))
        gup[...] = jnp.zeros(gup.shape, f32)
        gdown[...] = jnp.zeros(gdown.shape, f32)

        def tile(i, x):
            r = win(i * TILE)
            cv, dv = c[r, :], dm[r, :]
            e, du, mv, dcv = mlp_tile(cv, dv, up, down)
            m[r, :] = mv
            dc[r, :] = dcv
            gdown[...] += dot(e, dv, TN)
            gup[...] += dot(cv, du, TN)
            return x

        lax.fori_loop(0, n, tile, 0)
    return body


def hot_back(counts, line, s, patches):
    live = lax.broadcasted_iota(jnp.int32, (1, SLOTS), 1) < counts[s]
    pick = jnp.where(live, line[s, :, :SLOTS], -1)
    return (lax.broadcasted_iota(jnp.int32, (patches, SLOTS), 0) == pick).astype(f32).astype(bf16)


def mlp_other_body(samples, patches):
    def body(counts, line, c, dm, up, down, m, dc, r, gain, out, dr, g2, y):
        n = tiles(total_of(counts, samples))
        g2[...] = jnp.zeros(g2.shape, f32)

        def tile(i, x):
            rr = win(i * TILE)
            cv, dv = c[rr, :], dm[rr, :]
            _, _, mv, dcv = mlp_tile(cv, dv, up, down)
            rv = r[rr, :]
            y[rr, :] = (rv + (m[rr, :] + mv)).astype(bf16)
            dct = dc[rr, :] + dcv
            hat, inv = normed(rv)
            g2[0:1, :] += jnp.sum(dct * hat, axis=0, keepdims=True)
            g2[1:2, :] += jnp.sum(dct, axis=0, keepdims=True)
            dr[rr, :] = dv.astype(f32) + norm_back(dct, hat, inv, gain[...])
            return x

        lax.fori_loop(0, n, tile, 0)
        y[win(n * TILE), :] = jnp.zeros((TILE, y.shape[1]), bf16)

        def scatter(s, start):
            out[s] = dot(hot_back(counts, line, s, patches), y[win(start), :]).astype(bf16)
            return start + ((counts[s] + 15) // 16) * 16

        lax.fori_loop(0, samples, scatter, 0)
    return body


def attend_back(counts, qkv, do, lse, dqkv, samples, width):
    left = lane_halves()
    row = lax.broadcasted_iota(jnp.int32, (SLOTS, 1), 0)

    def one(s, start):
        rows = win(start)
        live = row < counts[s]
        for pair in range(width // 128):
            lo = pair * 128
            q = qkv[rows, lo:lo + 128]
            k = qkv[rows, width + lo:width + lo + 128]
            v = qkv[rows, 2 * width + lo:2 * width + lo + 128]
            dov = do[rows, lo:lo + 128]
            dov = jnp.where(live, dov, jnp.zeros_like(dov))
            zero = jnp.zeros_like(k)
            dq, dk, dvv = [], [], []
            for side in range(2):
                keep = left if side == 0 else ~left
                sc = dot(jnp.where(keep, k, zero), q, NT) * scale
                sc = jnp.where(live, sc, masked_score)
                p = jnp.exp(sc - lse[s, 2 * pair + side:2 * pair + side + 1, :])
                dp = dot(jnp.where(keep, v, zero), dov, NT)
                t = jnp.sum(p * dp, axis=0, keepdims=True)
                ds = (p * (dp - t)).astype(bf16)
                dq.append(dot(ds, k, TN))
                dk.append(dot(ds, q))
                dvv.append(dot(p.astype(bf16), dov))
            dqkv[rows, lo:lo + 128] = (jnp.where(left, dq[0], dq[1]) * scale).astype(bf16)
            dqkv[rows, width + lo:width + lo + 128] = (jnp.where(left, dk[0], dk[1]) * scale).astype(bf16)
            dqkv[rows, 2 * width + lo:2 * width + lo + 128] = jnp.where(left, dvv[0], dvv[1]).astype(bf16)
        return start + ((counts[s] + 15) // 16) * 16

    lax.fori_loop(0, samples, one, 0)


def attn_own_body(samples, width):
    def body(counts, dr, qkv, lse, o, a, wout, wqkv, da, gout, gqkv, do, dqkv):
        total = total_of(counts, samples)
        n = tiles(total)
        gout[...] = jnp.zeros(gout.shape, f32)
        gqkv[...] = jnp.zeros(gqkv.shape, f32)

        def first(i, x):
            r = win(i * TILE)
            dz = dr[r, :].astype(bf16)
            do[r, :] = dot(dz, wout[...], NT).astype(bf16)
            gout[...] += dot(o[r, :], dz, TN)
            return x

        lax.fori_loop(0, n, first, 0)
        attend_back(counts, qkv, do, lse, dqkv, samples, width)
        dqkv[win(total), :] = jnp.zeros((TILE, dqkv.shape[1]), bf16)

        def last(i, x):
            r = win(i * TILE)
            dv = dqkv[r, :]
            da[r, :] = dot(dv, wqkv[...], NT)
            for j in range(3):
                gqkv[j] += dot(a[r, :], dv[:, j * width:(j + 1) * width], TN)
            return x

        lax.fori_loop(0, n, last, 0)
    return body


def attn_other_body(samples, width, patches):
    def body(counts, line, dr, qkv, lse, wout, wqkv, da, h, gain, out, g1, do, dqkv, dh):
        total = total_of(counts, samples)
        n = tiles(total)
        g1[...] = jnp.zeros(g1.shape, f32)

        def first(i, x):
            r = win(i * TILE)
            do[r, :] = dot(dr[r, :].astype(bf16), wout[...], NT).astype(bf16)
            return x

        lax.fori_loop(0, n, first, 0)
        attend_back(counts, qkv, do, lse, dqkv, samples, width)
        dqkv[win(total), :] = jnp.zeros((TILE, dqkv.shape[1]), bf16)

        def last(i, x):
            r = win(i * TILE)
            dat = da[r, :] + dot(dqkv[r, :], wqkv[...], NT)
            hat, inv = normed(h[r, :].astype(f32))
            g1[0:1, :] += jnp.sum(dat * hat, axis=0, keepdims=True)
            g1[1:2, :] += jnp.sum(dat, axis=0, keepdims=True)
            dh[r, :] = (dr[r, :] + norm_back(dat, hat, inv, gain[...])).astype(bf16)
            return x

        lax.fori_loop(0, n, last, 0)
        dh[win(n * TILE), :] = jnp.zeros((TILE, dh.shape[1]), bf16)

        def scatter(s, start):
            out[s] = dot(hot_back(counts, line, s, patches), dh[win(start), :]).astype(bf16)
            return start + ((counts[s] + 15) // 16) * 16

        lax.fori_loop(0, samples, scatter, 0)
    return body


def sds(shape, dtype):
    return jax.ShapeDtypeStruct(shape, dtype)


def call(body, name, counts, args, outs, scratch=(), flops=0):
    moved = sum(x.size * x.dtype.itemsize for x in list(args) + list(outs))
    return pl.pallas_call(
        body,
        name=name,
        out_shape=list(outs),
        grid_spec=pltpu.PrefetchScalarGridSpec(
            num_scalar_prefetch=1,
            grid=(1,),
            in_specs=[pl.BlockSpec(x.shape, lambda i, n, d=x.ndim: (0,) * d, pipeline_mode=pl.Buffered(1)) for x in args],
            out_specs=[pl.BlockSpec(x.shape, lambda i, n, d=len(x.shape): (0,) * d, pipeline_mode=pl.Buffered(1)) for x in outs],
            scratch_shapes=list(scratch),
        ),
        compiler_params=pltpu.CompilerParams(vmem_limit_bytes=62 << 20),
        cost_estimate=pl.CostEstimate(flops=flops, transcendentals=0, bytes_accessed=moved),
    )(counts, *args)


def fwd_own(counts, col, patches, cot, gain, shift, weight):
    S, L, D = patches.shape
    width = weight.shape[1] // 3
    TP = S * SLOTS + TILE
    whole = lambda d: (lambda s, n: (0,) * d)
    one = lambda s, n: (s, 0, 0)
    B1 = pl.Buffered(1)
    outs = [sds((TP, D), bf16), sds((TP, D), bf16), sds((TP, D), bf16), sds((TP, 3 * width), bf16), sds((TP, width), bf16), sds((S, width // HD, SLOTS), f32)]
    return pl.pallas_call(
        fwd_own_body(S, width),
        name="fwd_own",
        out_shape=outs,
        grid_spec=pltpu.PrefetchScalarGridSpec(
            num_scalar_prefetch=1,
            grid=(S,),
            in_specs=[
                pl.BlockSpec((1, L, 1), one),
                pl.BlockSpec((1, L, D), one),
                pl.BlockSpec((1, L, D), one),
                pl.BlockSpec((1, D), whole(2)),
                pl.BlockSpec((1, D), whole(2)),
                pl.BlockSpec(weight.shape, whole(2), pipeline_mode=B1),
            ],
            out_specs=[pl.BlockSpec(x.shape, whole(len(x.shape)), pipeline_mode=B1) for x in outs],
        ),
        compiler_params=pltpu.CompilerParams(vmem_limit_bytes=62 << 20),
        cost_estimate=pl.CostEstimate(flops=6 * 10**9, transcendentals=0, bytes_accessed=25 << 20),
    )(counts, col, patches, cot, gain, shift, weight)


def fwd_other(counts, a, h, o, weight, out_own, out_other, gain, shift, S):
    TP, D = a.shape
    width = weight.shape[1] // 3
    outs = [sds((TP, 3 * width), bf16), sds((TP, width), bf16), sds((S, width // HD, SLOTS), f32), sds((TP, D), f32), sds((TP, D), bf16)]
    return call(fwd_other_body(S, width), "fwd_other", counts, [a, h, o, weight, out_own, out_other, gain, shift], outs, flops=7 * 10**9)


def mlp_own(counts, c, dm, up, down, S):
    TP, D = c.shape
    outs = [sds((TP, D), f32), sds((TP, D), f32), sds(up.shape, f32), sds(down.shape, f32)]
    return call(mlp_own_body(S), "mlp_own", counts, [c, dm, up, down], outs, flops=18 * 10**9)


def mlp_other(counts, line, c, dm, up, down, m, dc, r, gain, S, L):
    TP, D = c.shape
    outs = [sds((S, L, D), bf16), sds((TP, D), f32), sds((8, D), f32)]
    return call(mlp_other_body(S, L), "mlp_other", counts, [line, c, dm, up, down, m, dc, r, gain], outs, [pltpu.VMEM((TP, D), bf16)], flops=12 * 10**9)


def attn_own(counts, dr, qkv, lse, o, a, wout, wqkv, S):
    TP, D = a.shape
    width = wout.shape[0]
    outs = [sds((TP, D), f32), sds(wout.shape, f32), sds((3, D, width), f32)]
    return call(attn_own_body(S, width), "attn_own", counts, [dr, qkv, lse, o, a, wout, wqkv], outs, [pltpu.VMEM((TP, width), bf16), pltpu.VMEM((TP, 3 * width), bf16)], flops=9 * 10**9)


def attn_other(counts, line, dr, qkv, lse, wout, wqkv, da, h, gain, S, L):
    TP, D = h.shape
    width = wout.shape[0]
    outs = [sds((S, L, D), bf16), sds((8, D), f32)]
    return call(attn_other_body(S, width, L), "attn_other", counts, [line, dr, qkv, lse, wout, wqkv, da, h, gain], outs, [pltpu.VMEM((TP, width), bf16), pltpu.VMEM((TP, 3 * width), bf16), pltpu.VMEM((TP, D), bf16)], flops=8 * 10**9)


def swap(x, axis, size, bit):
    return lax.ppermute(x, axis, [(k, k ^ bit) for k in range(size)])


def tie(*xs):
    return lax.optimization_barrier(xs)


def cast_pieces(order, pieces):
    rows, cols = pieces[0].shape

    def body(where, *refs):
        for i in range(4):
            refs[4][pl.ds(pl.multiple_of(where[i] * rows, 16), rows), :] = refs[i][...].astype(bf16)

    return call(body, "cast_pieces", order, pieces, [sds((4 * rows, cols), bf16)])[0]


def side(bit):
    return (lax.axis_index("dp") // bit) % 2


def half(x, i):
    n = x.shape[0] // 2
    return lax.dynamic_slice_in_dim(x, i * n, n, 0)


def fold(x, bit, dp):
    i = side(bit)
    return half(x, i) + swap(half(x, 1 - i), "dp", dp, bit)


def spread(x, bit, dp):
    got = swap(x, "dp", dp, bit)
    first = side(bit) == 0
    return jnp.concatenate([jnp.where(first, x, got), jnp.where(first, got, x)], 0)


def folds(x, bits, dp):
    for bit in bits:
        x = fold(x, bit, dp)
    return x


def spreads(x, bits, dp):
    for bit in reversed(bits):
        x = spread(x, bit, dp)
    return x


def shards(dp, patches, counts, visible, g1, b1, wq, wo, g2, b2, wu, wd, cot):
    S, L, D = patches.shape
    wt = wq.transpose(1, 0, 2)
    wq = jnp.concatenate([wt[0], wt[1], wt[2]], axis=1)
    col, line = visible[:, :, None], visible[:, None, :]
    g1, b1, g2, b2 = (x[None, :] for x in (g1, b1, g2, b2))
    me = lax.axis_index("dp") % 4
    order = jnp.stack([me, me ^ 2, me ^ 1, me ^ 3]).astype(jnp.int32)

    def part(w):
        rows = w.shape[0] // 4
        return lax.dynamic_slice_in_dim(w, me * rows, rows, 0).astype(f32)

    def rest(first, across):
        return cast_pieces(order, [first, across, swap(first, "dp", dp, 1), swap(across, "dp", dp, 1)])

    every = [1 << i for i in range(dp.bit_length() - 1)]
    along = every
    other = [1, 4, 2] + every[3:] if len(every) > 2 else every

    fq, fo = swap(part(wq), "tensor", 2, 1), swap(part(wo), "tensor", 2, 1)
    h, dm, a, qkv0, o0, lse0 = fwd_own(counts, col, patches, cot, g1, b1, wq)
    fq, fo, pu, pd, a = tie(fq, fo, part(wu), part(wd), a)
    aq, ao = swap(fq, "dp", dp, 2), swap(fo, "dp", dp, 2)
    fu, fd = swap(pu, "tensor", 2, 1), swap(pd, "tensor", 2, 1)
    wq1, wo1 = rest(fq, aq), rest(fo, ao)
    qkv1, o1, lse1, r, c = fwd_other(counts, a, h, o0, wq1, wo, wo1, g2, b2, S)
    fu, fd, c = tie(fu, fd, c)
    au, ad = swap(fu, "dp", dp, 2), swap(fd, "dp", dp, 2)
    m, dc, gup, gdown = mlp_own(counts, c, dm, wu, wd, S)
    au, ad, m = tie(au, ad, m)
    wu1, wd1 = rest(fu, au), rest(fd, ad)
    A, B = fold(gup, 1, dp), fold(gdown, 1, dp)
    A, B, c = tie(A, B, c)
    out, dr, gg2 = mlp_other(counts, line, c, dm, wu1, wd1, m, dc, r, g2, S, L)
    A, B = fold(A, along[1], dp), fold(B, other[1], dp)
    A, B, dr = tie(A, B, dr)
    A, B = fold(A, along[2], dp), fold(B, other[2], dp)
    da, gout, gqkv = attn_own(counts, dr, qkv0, lse0, o0, a, wo, wq, S)
    A, B, da = tie(A, B, da)
    A, B = folds(A, along[3:], dp), folds(B, other[3:], dp)
    C, E = fold(gqkv.reshape(3 * D, -1), 1, dp), fold(gout, 1, dp)
    gin, gg1 = attn_other(counts, line, dr, qkv1, lse1, wo1, wq1, da, h, g1, S, L)
    C, E, A, B, gg1 = tie(C, E, A, B, gg1)
    small = jnp.concatenate([gg1, gg2], 0)
    for bit in every:
        small = small + swap(small, "dp", dp, bit)
    gg1, gg2 = small[:8], small[8:]
    gup, gdown = spreads(A, along, dp), spreads(B, other, dp)
    gqkv = spreads(folds(C, along[1:], dp), along, dp).reshape(3, D, -1)
    gout = spreads(folds(E, other[1:], dp), other, dp)
    return (out, gin, gg1[0], gg1[1], gqkv.transpose(1, 0, 2), gout, gg2[0], gg2[1], gup, gdown)


def solution(mesh):
    dp = mesh.shape["dp"]
    placed = (P("dp", None, None), P("dp"), P("dp", None), P(), P(), P(None, None, "tensor"), P("tensor", None), P(), P(), P(None, "tensor"), P("tensor", None), P("dp", None, None))
    outs = (P("dp", None, None), P("dp", None, None), P(), P(), P(None, None, "tensor"), P("tensor", None), P(), P(), P(None, "tensor"), P("tensor", None))
    return jax.shard_map(lambda *a: shards(dp, *a), mesh=mesh, in_specs=placed, out_specs=outs, check_vma=False)
```

```python
import jax
import jax.numpy as jnp
from jax import lax
from jax.sharding import PartitionSpec as P
from jax.experimental import pallas as pl
from jax.experimental.pallas import tpu as pltpu

HD = 64
SLOTS = 256
TILE = 256
norm_eps = 1e-06
masked_score = -1e30
scale = HD ** (-0.5)
f32, bf16 = jnp.float32, jnp.bfloat16


def dot(x, y, dims=((1,), (0,))):
    return lax.dot_general(x, y, (dims, ((), ())), preferred_element_type=f32)


NT = ((1,), (1,))
TN = ((0,), (0,))


def win(start, size=SLOTS):
    if not isinstance(start, int):
        start = pl.multiple_of(start, 16)
    return pl.ds(start, size)


def start_of(counts, s):
    return lax.fori_loop(0, s, lambda i, t: t + ((counts[i] + 15) // 16) * 16, 0)


def total_of(counts, samples):
    return start_of(counts, samples)


def normed(values):
    center = values - jnp.mean(values, axis=-1, keepdims=True)
    spread = jnp.mean(center * center, axis=-1, keepdims=True)
    inv = lax.rsqrt(spread + norm_eps)
    return center * inv, inv


def norm_back(grad, hat, inv, gain):
    g = grad * gain
    return inv * (g - jnp.mean(g, axis=-1, keepdims=True) - hat * jnp.mean(g * hat, axis=-1, keepdims=True))


def lane_halves():
    lane = lax.broadcasted_iota(jnp.int32, (1, 128), 1)
    return lane < HD


def attend_rows(counts, qkv, out, lse, samples, width):
    left = lane_halves()
    row = lax.broadcasted_iota(jnp.int32, (SLOTS, 1), 0)

    def one(s, start):
        rows = win(start)
        live = row < counts[s]
        for pair in range(width // 128):
            lo = pair * 128
            q = qkv[rows, lo:lo + 128]
            k = qkv[rows, width + lo:width + lo + 128]
            v = qkv[rows, 2 * width + lo:2 * width + lo + 128]
            parts = []
            for side in range(2):
                keep = left if side == 0 else ~left
                sc = dot(jnp.where(keep, k, jnp.zeros_like(k)), q, NT) * scale
                sc = jnp.where(live, sc, masked_score)
                top = jnp.max(sc, axis=0, keepdims=True)
                w = jnp.exp(sc - top)
                tot = jnp.sum(w, axis=0, keepdims=True)
                lse[s, 2 * pair + side:2 * pair + side + 1, :] = top + jnp.log(tot)
                p = (w * (1.0 / tot)).astype(bf16)
                parts.append(dot(p, v, TN))
            out[rows, lo:lo + 128] = jnp.where(left, parts[0], parts[1]).astype(bf16)
        return start + ((counts[s] + 15) // 16) * 16

    lax.fori_loop(0, samples, one, 0)


def tiles(total):
    return (total + TILE - 1) // TILE


def fwd_own_body(samples, width):
    def body(counts, col, patches, cot, gain, shift, weight, h, dm, a, qkv, o, lse):
        s = pl.program_id(0)
        start = start_of(counts, s)
        pick = col[0, :SLOTS, :]
        row = lax.broadcasted_iota(jnp.int32, (SLOTS, 1), 0)
        pick = jnp.where(row < counts[s], pick, -1)
        hot = (lax.broadcasted_iota(jnp.int32, (SLOTS, patches.shape[1]), 1) == pick).astype(f32).astype(bf16)
        h[win(start), :] = dot(hot, patches[0]).astype(bf16)
        dm[win(start), :] = dot(hot, cot[0]).astype(bf16)

        @pl.when(s == samples - 1)
        def _():
            total = total_of(counts, samples)
            zeros = jnp.zeros((TILE, h.shape[1]), bf16)
            h[win(total), :] = zeros
            dm[win(total), :] = zeros

            def tile(i, c):
                r = win(i * TILE)
                hat, _ = normed(h[r, :].astype(f32))
                av = (hat * gain[...] + shift[...]).astype(bf16)
                a[r, :] = av
                qkv[r, :] = dot(av, weight[...]).astype(bf16)
                return c

            n = tiles(total)
            lax.fori_loop(0, n, tile, 0)
            qkv[win(n * TILE), :] = jnp.zeros((TILE, qkv.shape[1]), bf16)
            attend_rows(counts, qkv, o, lse, samples, width)
            o[win(total), :] = jnp.zeros((TILE, width), bf16)

    return body


def fwd_other_body(samples, width):
    def body(counts, a, h, o, weight, out_own, out_other, gain, shift, qkv, o2, lse, r, c):
        total = total_of(counts, samples)
        n = tiles(total)

        def tile(i, x):
            rr = win(i * TILE)
            qkv[rr, :] = dot(a[rr, :], weight[...]).astype(bf16)
            return x

        lax.fori_loop(0, n, tile, 0)
        qkv[win(n * TILE), :] = jnp.zeros((TILE, qkv.shape[1]), bf16)
        attend_rows(counts, qkv, o2, lse, samples, width)
        o2[win(total), :] = jnp.zeros((TILE, width), bf16)

        def tail(i, x):
            rr = win(i * TILE)
            z = dot(o[rr, :], out_own[...]) + dot(o2[rr, :], out_other[...])
            rv = h[rr, :].astype(f32) + z
            r[rr, :] = rv
            hat, _ = normed(rv)
            c[rr, :] = (hat * gain[...] + shift[...]).astype(bf16)
            return x

        lax.fori_loop(0, n, tail, 0)

    return body


def gelu_both(u):
    cdf = 0.5 * (1.0 + lax.erf(u * (0.5 ** 0.5)))
    pdf = jnp.exp(-0.5 * u * u) * (0.5 / jnp.pi) ** 0.5
    return u * cdf, cdf + u * pdf


def mlp_tile(cv, dv, up, down):
    u = dot(cv, up[...])
    e, slope = gelu_both(u)
    e = e.astype(bf16)
    m = dot(e, down[...])
    de = dot(dv, down[...], NT)
    du = (de * slope).astype(bf16)
    dc = dot(du, up[...], NT)
    return e, du, m, dc


def mlp_own_body(samples):
    def body(counts, c, dm, up, down, m, dc, gup, gdown):
        n = tiles(total_of(counts, samples))
        gup[...] = jnp.zeros(gup.shape, f32)
        gdown[...] = jnp.zeros(gdown.shape, f32)

        def tile(i, x):
            r = win(i * TILE)
            cv, dv = c[r, :], dm[r, :]
            e, du, mv, dcv = mlp_tile(cv, dv, up, down)
            m[r, :] = mv
            dc[r, :] = dcv
            gdown[...] += dot(e, dv, TN)
            gup[...] += dot(cv, du, TN)
            return x

        lax.fori_loop(0, n, tile, 0)

    return body


def hot_back(counts, line, s, patches):
    live = lax.broadcasted_iota(jnp.int32, (1, SLOTS), 1) < counts[s]
    pick = jnp.where(live, line[s, :, :SLOTS], -1)
    return (lax.broadcasted_iota(jnp.int32, (patches, SLOTS), 0) == pick).astype(f32).astype(bf16)


def mlp_other_body(samples, patches):
    def body(counts, line, c, dm, up, down, m, dc, r, gain, out, dr, g2, y):
        n = tiles(total_of(counts, samples))
        g2[...] = jnp.zeros(g2.shape, f32)

        def tile(i, x):
            rr = win(i * TILE)
            cv, dv = c[rr, :], dm[rr, :]
            _, _, mv, dcv = mlp_tile(cv, dv, up, down)
            rv = r[rr, :]
            y[rr, :] = (rv + (m[rr, :] + mv)).astype(bf16)
            dct = dc[rr, :] + dcv
            hat, inv = normed(rv)
            g2[0:1, :] += jnp.sum(dct * hat, axis=0, keepdims=True)
            g2[1:2, :] += jnp.sum(dct, axis=0, keepdims=True)
            dr[rr, :] = dv.astype(f32) + norm_back(dct, hat, inv, gain[...])
            return x

        lax.fori_loop(0, n, tile, 0)
        y[win(n * TILE), :] = jnp.zeros((TILE, y.shape[1]), bf16)

        def scatter(s, start):
            out[s] = dot(hot_back(counts, line, s, patches), y[win(start), :]).astype(bf16)
            return start + ((counts[s] + 15) // 16) * 16

        lax.fori_loop(0, samples, scatter, 0)

    return body


def attend_back(counts, qkv, do, lse, dqkv, samples, width):
    left = lane_halves()
    row = lax.broadcasted_iota(jnp.int32, (SLOTS, 1), 0)

    def one(s, start):
        rows = win(start)
        live = row < counts[s]
        for pair in range(width // 128):
            lo = pair * 128
            q = qkv[rows, lo:lo + 128]
            k = qkv[rows, width + lo:width + lo + 128]
            v = qkv[rows, 2 * width + lo:2 * width + lo + 128]
            dov = do[rows, lo:lo + 128]
            dov = jnp.where(live, dov, jnp.zeros_like(dov))
            zero = jnp.zeros_like(k)
            dq, dk, dvv = [], [], []
            for side in range(2):
                keep = left if side == 0 else ~left
                sc = dot(jnp.where(keep, k, zero), q, NT) * scale
                sc = jnp.where(live, sc, masked_score)
                p = jnp.exp(sc - lse[s, 2 * pair + side:2 * pair + side + 1, :])
                dp = dot(jnp.where(keep, v, zero), dov, NT)
                t = jnp.sum(p * dp, axis=0, keepdims=True)
                ds = (p * (dp - t)).astype(bf16)
                dq.append(dot(ds, k, TN))
                dk.append(dot(ds, q))
                dvv.append(dot(p.astype(bf16), dov))
            dqkv[rows, lo:lo + 128] = (jnp.where(left, dq[0], dq[1]) * scale).astype(bf16)
            dqkv[rows, width + lo:width + lo + 128] = (jnp.where(left, dk[0], dk[1]) * scale).astype(bf16)
            dqkv[rows, 2 * width + lo:2 * width + lo + 128] = jnp.where(left, dvv[0], dvv[1]).astype(bf16)
        return start + ((counts[s] + 15) // 16) * 16

    lax.fori_loop(0, samples, one, 0)


def attn_own_body(samples, width):
    def body(counts, dr, qkv, lse, o, a, wout, wqkv, da, gout, gqkv, do, dqkv):
        total = total_of(counts, samples)
        n = tiles(total)
        gout[...] = jnp.zeros(gout.shape, f32)
        gqkv[...] = jnp.zeros(gqkv.shape, f32)

        def first(i, x):
            r = win(i * TILE)
            dz = dr[r, :].astype(bf16)
            do[r, :] = dot(dz, wout[...], NT).astype(bf16)
            gout[...] += dot(o[r, :], dz, TN)
            return x

        lax.fori_loop(0, n, first, 0)
        attend_back(counts, qkv, do, lse, dqkv, samples, width)
        dqkv[win(total), :] = jnp.zeros((TILE, dqkv.shape[1]), bf16)

        def last(i, x):
            r = win(i * TILE)
            dv = dqkv[r, :]
            da[r, :] = dot(dv, wqkv[...], NT)
            for j in range(3):
                gqkv[j] += dot(a[r, :], dv[:, j * width:(j + 1) * width], TN)
            return x

        lax.fori_loop(0, n, last, 0)

    return body


def attn_other_body(samples, width, patches):
    def body(counts, line, dr, qkv, lse, wout, wqkv, da, h, gain, out, g1, do, dqkv, dh):
        total = total_of(counts, samples)
        n = tiles(total)
        g1[...] = jnp.zeros(g1.shape, f32)

        def first(i, x):
            r = win(i * TILE)
            do[r, :] = dot(dr[r, :].astype(bf16), wout[...], NT).astype(bf16)
            return x

        lax.fori_loop(0, n, first, 0)
        attend_back(counts, qkv, do, lse, dqkv, samples, width)
        dqkv[win(total), :] = jnp.zeros((TILE, dqkv.shape[1]), bf16)

        def last(i, x):
            r = win(i * TILE)
            dat = da[r, :] + dot(dqkv[r, :], wqkv[...], NT)
            hat, inv = normed(h[r, :].astype(f32))
            g1[0:1, :] += jnp.sum(dat * hat, axis=0, keepdims=True)
            g1[1:2, :] += jnp.sum(dat, axis=0, keepdims=True)
            dh[r, :] = (dr[r, :] + norm_back(dat, hat, inv, gain[...])).astype(bf16)
            return x

        lax.fori_loop(0, n, last, 0)
        dh[win(n * TILE), :] = jnp.zeros((TILE, dh.shape[1]), bf16)

        def scatter(s, start):
            out[s] = dot(hot_back(counts, line, s, patches), dh[win(start), :]).astype(bf16)
            return start + ((counts[s] + 15) // 16) * 16

        lax.fori_loop(0, samples, scatter, 0)

    return body


def sds(shape, dtype):
    return jax.ShapeDtypeStruct(shape, dtype)


def call(body, counts, args, outs, scratch=(), flops=0):
    moved = sum(x.size * x.dtype.itemsize for x in list(args) + list(outs))
    return pl.pallas_call(
        body,
        out_shape=list(outs),
        grid_spec=pltpu.PrefetchScalarGridSpec(
            num_scalar_prefetch=1,
            grid=(1,),
            in_specs=[pl.BlockSpec(x.shape, lambda i, n, d=x.ndim: (0,) * d, pipeline_mode=pl.Buffered(1)) for x in args],
            out_specs=[pl.BlockSpec(x.shape, lambda i, n, d=len(x.shape): (0,) * d, pipeline_mode=pl.Buffered(1)) for x in outs],
            scratch_shapes=list(scratch),
        ),
        compiler_params=pltpu.CompilerParams(vmem_limit_bytes=62 << 20),
        cost_estimate=pl.CostEstimate(flops=flops, transcendentals=0, bytes_accessed=moved),
    )(counts, *args)


def fwd_own(counts, col, patches, cot, gain, shift, weight):
    S, L, D = patches.shape
    width = weight.shape[1] // 3
    TP = S * SLOTS + TILE
    whole = lambda d: (lambda s, n: (0,) * d)
    one = lambda s, n: (s, 0, 0)
    B1 = pl.Buffered(1)
    outs = [sds((TP, D), bf16), sds((TP, D), bf16), sds((TP, D), bf16), sds((TP, 3 * width), bf16), sds((TP, width), bf16), sds((S, width // HD, SLOTS), f32)]
    return pl.pallas_call(
        fwd_own_body(S, width),
        name="fwd_own",
        out_shape=outs,
        grid_spec=pltpu.PrefetchScalarGridSpec(
            num_scalar_prefetch=1,
            grid=(S,),
            in_specs=[
                pl.BlockSpec((1, L, 1), one),
                pl.BlockSpec((1, L, D), one),
                pl.BlockSpec((1, L, D), one),
                pl.BlockSpec((1, D), whole(2)),
                pl.BlockSpec((1, D), whole(2)),
                pl.BlockSpec(weight.shape, whole(2), pipeline_mode=B1),
            ],
            out_specs=[pl.BlockSpec(x.shape, whole(len(x.shape)), pipeline_mode=B1) for x in outs],
        ),
        compiler_params=pltpu.CompilerParams(vmem_limit_bytes=62 << 20),
        cost_estimate=pl.CostEstimate(flops=6 * 10**9, transcendentals=0, bytes_accessed=25 << 20),
    )(counts, col, patches, cot, gain, shift, weight)


def fwd_other(counts, a, h, o, weight, out_own, out_other, gain, shift, S):
    TP, D = a.shape
    width = weight.shape[1] // 3
    outs = [sds((TP, 3 * width), bf16), sds((TP, width), bf16), sds((S, width // HD, SLOTS), f32), sds((TP, D), f32), sds((TP, D), bf16)]
    return call(fwd_other_body(S, width), counts, [a, h, o, weight, out_own, out_other, gain, shift], outs, flops=7 * 10**9)


def mlp_own(counts, c, dm, up, down, S):
    TP, D = c.shape
    outs = [sds((TP, D), f32), sds((TP, D), f32), sds(up.shape, f32), sds(down.shape, f32)]
    return call(mlp_own_body(S), counts, [c, dm, up, down], outs, flops=18 * 10**9)


def mlp_other(counts, line, c, dm, up, down, m, dc, r, gain, S, L):
    TP, D = c.shape
    outs = [sds((S, L, D), bf16), sds((TP, D), f32), sds((8, D), f32)]
    return call(mlp_other_body(S, L), counts, [line, c, dm, up, down, m, dc, r, gain], outs, [pltpu.VMEM((TP, D), bf16)], flops=12 * 10**9)


def attn_own(counts, dr, qkv, lse, o, a, wout, wqkv, S):
    TP, D = a.shape
    width = wout.shape[0]
    outs = [sds((TP, D), f32), sds(wout.shape, f32), sds((3, D, width), f32)]
    return call(attn_own_body(S, width), counts, [dr, qkv, lse, o, a, wout, wqkv], outs, [pltpu.VMEM((TP, width), bf16), pltpu.VMEM((TP, 3 * width), bf16)], flops=9 * 10**9)


def attn_other(counts, line, dr, qkv, lse, wout, wqkv, da, h, gain, S, L):
    TP, D = h.shape
    width = wout.shape[0]
    outs = [sds((S, L, D), bf16), sds((8, D), f32)]
    return call(attn_other_body(S, width, L), counts, [line, dr, qkv, lse, wout, wqkv, da, h, gain], outs, [pltpu.VMEM((TP, width), bf16), pltpu.VMEM((TP, 3 * width), bf16), pltpu.VMEM((TP, D), bf16)], flops=8 * 10**9)


def swap(x, axis, size, bit):
    return lax.ppermute(x, axis, [(k, k ^ bit) for k in range(size)])


def tie(*xs):
    return lax.optimization_barrier(xs)


def cast_pieces(order, pieces):
    rows, cols = pieces[0].shape

    def body(where, *refs):
        for i in range(4):
            refs[4][pl.ds(pl.multiple_of(where[i] * rows, 16), rows), :] = refs[i][...].astype(bf16)

    return call(body, order, pieces, [sds((4 * rows, cols), bf16)])[0]


def side(bit):
    return (lax.axis_index("dp") // bit) % 2


def half(x, i):
    n = x.shape[0] // 2
    return lax.dynamic_slice_in_dim(x, i * n, n, 0)


def fold(x, bit, dp):
    i = side(bit)
    return half(x, i) + swap(half(x, 1 - i), "dp", dp, bit)


def spread(x, bit, dp):
    got = swap(x, "dp", dp, bit)
    first = side(bit) == 0
    return jnp.concatenate([jnp.where(first, x, got), jnp.where(first, got, x)], 0)


def folds(x, bits, dp):
    for bit in bits:
        x = fold(x, bit, dp)
    return x


def spreads(x, bits, dp):
    for bit in reversed(bits):
        x = spread(x, bit, dp)
    return x


def shards(dp, patches, counts, visible, g1, b1, wq, wo, g2, b2, wu, wd, cot):
    S, L, D = patches.shape
    wt = wq.transpose(1, 0, 2)
    wq = jnp.concatenate([wt[0], wt[1], wt[2]], axis=1)
    col, line = visible[:, :, None], visible[:, None, :]
    g1, b1, g2, b2 = (x[None, :] for x in (g1, b1, g2, b2))
    me = lax.axis_index("dp") % 4
    order = jnp.stack([me, me ^ 2, me ^ 1, me ^ 3]).astype(jnp.int32)

    def part(w):
        rows = w.shape[0] // 4
        return lax.dynamic_slice_in_dim(w, me * rows, rows, 0).astype(f32)

    def rest(first, across):
        return cast_pieces(order, [first, across, swap(first, "dp", dp, 1), swap(across, "dp", dp, 1)])

    every = [1 << i for i in range(dp.bit_length() - 1)]
    along = every
    other = [1, 4, 2] + every[3:] if len(every) > 2 else every

    fq, fo = swap(part(wq), "tensor", 2, 1), swap(part(wo), "tensor", 2, 1)
    h, dm, a, qkv0, o0, lse0 = fwd_own(counts, col, patches, cot, g1, b1, wq)
    fq, fo, pu, pd, a = tie(fq, fo, part(wu), part(wd), a)
    aq, ao = swap(fq, "dp", dp, 2), swap(fo, "dp", dp, 2)
    fu, fd = swap(pu, "tensor", 2, 1), swap(pd, "tensor", 2, 1)
    wq1, wo1 = rest(fq, aq), rest(fo, ao)
    qkv1, _, lse1, r, c = fwd_other(counts, a, h, o0, wq1, wo, wo1, g2, b2, S)
    fu, fd, c = tie(fu, fd, c)
    au = swap(fu, "dp", dp, 2)
    ad = swap(fd, "dp", dp, 2)
    m, dc, gup, gdown = mlp_own(counts, c, dm, wu, wd, S)
    au, ad, m = tie(au, ad, m)
    wu1, wd1 = rest(fu, au), rest(fd, ad)
    A, B = fold(gup, 1, dp), fold(gdown, 1, dp)
    A, B, c = tie(A, B, c)
    out, dr, gg2 = mlp_other(counts, line, c, dm, wu1, wd1, m, dc, r, g2, S, L)
    A, B = fold(A, along[1], dp), fold(B, other[1], dp)
    A, B, dr = tie(A, B, dr)
    A, B = fold(A, along[2], dp), fold(B, other[2], dp)
    da, gout, gqkv = attn_own(counts, dr, qkv0, lse0, o0, a, wo, wq, S)
    A, B, da = tie(A, B, da)
    A, B = folds(A, along[3:], dp), folds(B, other[3:], dp)
    C = gqkv.reshape(2, (3 * D) // 2, -1)
    C, F, E = fold(C[0], 1, dp), fold(C[1], 1, dp), fold(gout, 1, dp)
    gin, gg1 = attn_other(counts, line, dr, qkv1, lse1, wo1, wq1, da, h, g1, S, L)
    C, F, E, A, B, gg1 = tie(C, F, E, A, B, gg1)
    small = jnp.concatenate([gg1, gg2], 0)
    for bit, late in zip(reversed(along), reversed(other)):
        A, B = spread(A, bit, dp), spread(B, late, dp)
        small = small + swap(small, "dp", dp, bit)
        if bit != 1:
            A, B, small = tie(A, B, small)
    gup, gdown = A, B
    gg1, gg2 = small[:8], small[8:]
    C = spreads(folds(C, along[1:], dp), along, dp)
    F = spreads(folds(F, other[1:], dp), other, dp)
    gqkv = jnp.concatenate([C, F], 0).reshape(3, D, -1)
    gout = spreads(folds(E, other[1:], dp), other, dp)
    return (out, gin, gg1[0], gg1[1], gqkv.transpose(1, 0, 2), gout, gg2[0], gg2[1], gup, gdown)


def solution(mesh):
    dp = mesh.shape["dp"]
    placed = (P("dp", None, None), P("dp"), P("dp", None), P(), P(), P(None, None, "tensor"), P("tensor", None), P(), P(), P(None, "tensor"), P("tensor", None), P("dp", None, None))
    outs = (P("dp", None, None), P("dp", None, None), P(), P(), P(None, None, "tensor"), P("tensor", None), P(), P(), P(None, "tensor"), P("tensor", None))

    def layer(*a):
        return shards(dp, *a)

    return jax.shard_map(layer, mesh=mesh, in_specs=placed, out_specs=outs, check_vma=False)
```

```python
import jax
import jax.numpy as jnp
from jax import lax
from jax.sharding import PartitionSpec as P
from jax.experimental import pallas as pl
from jax.experimental.pallas import tpu as pltpu

HD = 64
SLOTS = 256
TILE = 256
norm_eps = 1e-06
masked_score = -1e30
scale = HD ** (-0.5)
f32, bf16 = jnp.float32, jnp.bfloat16


def dot(x, y, dims=((1,), (0,))):
    return lax.dot_general(x, y, (dims, ((), ())), preferred_element_type=f32)


NT = ((1,), (1,))
TN = ((0,), (0,))


def win(start, size=SLOTS):
    if not isinstance(start, int):
        start = pl.multiple_of(start, 16)
    return pl.ds(start, size)


def start_of(counts, s):
    return lax.fori_loop(0, s, lambda i, t: t + ((counts[i] + 15) // 16) * 16, 0)


def total_of(counts, samples):
    return start_of(counts, samples)


def normed(values):
    center = values - jnp.mean(values, axis=-1, keepdims=True)
    spread = jnp.mean(center * center, axis=-1, keepdims=True)
    inv = lax.rsqrt(spread + norm_eps)
    return center * inv, inv


def norm_back(grad, hat, inv, gain):
    g = grad * gain
    return inv * (g - jnp.mean(g, axis=-1, keepdims=True) - hat * jnp.mean(g * hat, axis=-1, keepdims=True))


def lane_halves():
    lane = lax.broadcasted_iota(jnp.int32, (1, 128), 1)
    return lane < HD


def attend_rows(counts, qkv, out, lse, samples, width):
    left = lane_halves()
    row = lax.broadcasted_iota(jnp.int32, (SLOTS, 1), 0)

    def one(s, start):
        rows = win(start)
        live = row < counts[s]
        for pair in range(width // 128):
            lo = pair * 128
            q = qkv[rows, lo:lo + 128]
            k = qkv[rows, width + lo:width + lo + 128]
            v = qkv[rows, 2 * width + lo:2 * width + lo + 128]
            parts = []
            for side in range(2):
                keep = left if side == 0 else ~left
                sc = dot(jnp.where(keep, k, jnp.zeros_like(k)), q, NT) * scale
                sc = jnp.where(live, sc, masked_score)
                top = jnp.max(sc, axis=0, keepdims=True)
                w = jnp.exp(sc - top)
                tot = jnp.sum(w, axis=0, keepdims=True)
                lse[s, 2 * pair + side:2 * pair + side + 1, :] = top + jnp.log(tot)
                p = (w * (1.0 / tot)).astype(bf16)
                parts.append(dot(p, v, TN))
            out[rows, lo:lo + 128] = jnp.where(left, parts[0], parts[1]).astype(bf16)
        return start + ((counts[s] + 15) // 16) * 16

    lax.fori_loop(0, samples, one, 0)


def tiles(total):
    return (total + TILE - 1) // TILE


def fwd_own_body(samples, width):
    def body(counts, col, patches, cot, gain, shift, weight, h, dm, a, qkv, o, lse):
        s = pl.program_id(0)
        start = start_of(counts, s)
        pick = col[0, :SLOTS, :]
        row = lax.broadcasted_iota(jnp.int32, (SLOTS, 1), 0)
        pick = jnp.where(row < counts[s], pick, -1)
        hot = (lax.broadcasted_iota(jnp.int32, (SLOTS, patches.shape[1]), 1) == pick).astype(f32).astype(bf16)
        h[win(start), :] = dot(hot, patches[0]).astype(bf16)
        dm[win(start), :] = dot(hot, cot[0]).astype(bf16)

        @pl.when(s == samples - 1)
        def _():
            total = total_of(counts, samples)
            zeros = jnp.zeros((TILE, h.shape[1]), bf16)
            h[win(total), :] = zeros
            dm[win(total), :] = zeros

            def tile(i, c):
                r = win(i * TILE)
                hat, _ = normed(h[r, :].astype(f32))
                av = (hat * gain[...] + shift[...]).astype(bf16)
                a[r, :] = av
                qkv[r, :] = dot(av, weight[...]).astype(bf16)
                return c

            n = tiles(total)
            lax.fori_loop(0, n, tile, 0)
            qkv[win(n * TILE), :] = jnp.zeros((TILE, qkv.shape[1]), bf16)
            attend_rows(counts, qkv, o, lse, samples, width)
            o[win(total), :] = jnp.zeros((TILE, width), bf16)

    return body


def join(counts, samples, pieces, full):
    rows = pieces[0].shape[0]
    for i in range(4):
        full[pl.ds(pl.multiple_of(counts[samples + i] * rows, 16), rows), :] = pieces[i][...].astype(bf16)


def fwd_other_body(samples, width):
    def body(counts, a, h, o, q0, q1, q2, q3, w0, w1, w2, w3, out_own, gain, shift, qkv, o2, lse, r, c, weight, out_other):
        join(counts, samples, (q0, q1, q2, q3), weight)
        join(counts, samples, (w0, w1, w2, w3), out_other)
        total = total_of(counts, samples)
        n = tiles(total)

        def tile(i, x):
            rr = win(i * TILE)
            qkv[rr, :] = dot(a[rr, :], weight[...]).astype(bf16)
            return x

        lax.fori_loop(0, n, tile, 0)
        qkv[win(n * TILE), :] = jnp.zeros((TILE, qkv.shape[1]), bf16)
        attend_rows(counts, qkv, o2, lse, samples, width)
        o2[win(total), :] = jnp.zeros((TILE, width), bf16)

        def tail(i, x):
            rr = win(i * TILE)
            z = dot(o[rr, :], out_own[...]) + dot(o2[rr, :], out_other[...])
            rv = h[rr, :].astype(f32) + z
            r[rr, :] = rv
            hat, _ = normed(rv)
            c[rr, :] = (hat * gain[...] + shift[...]).astype(bf16)
            return x

        lax.fori_loop(0, n, tail, 0)

    return body


def gelu_both(u):
    cdf = 0.5 * (1.0 + lax.erf(u * (0.5 ** 0.5)))
    pdf = jnp.exp(-0.5 * u * u) * (0.5 / jnp.pi) ** 0.5
    return u * cdf, cdf + u * pdf


def mlp_tile(cv, dv, up, down):
    u = dot(cv, up[...])
    e, slope = gelu_both(u)
    e = e.astype(bf16)
    m = dot(e, down[...])
    de = dot(dv, down[...], NT)
    du = (de * slope).astype(bf16)
    dc = dot(du, up[...], NT)
    return e, du, m, dc


def mlp_own_body(samples):
    def body(counts, c, dm, up, down, m, dc, gup, gdown):
        n = tiles(total_of(counts, samples))
        gup[...] = jnp.zeros(gup.shape, f32)
        gdown[...] = jnp.zeros(gdown.shape, f32)

        def tile(i, x):
            r = win(i * TILE)
            cv, dv = c[r, :], dm[r, :]
            e, du, mv, dcv = mlp_tile(cv, dv, up, down)
            m[r, :] = mv
            dc[r, :] = dcv
            gdown[...] += dot(e, dv, TN)
            gup[...] += dot(cv, du, TN)
            return x

        lax.fori_loop(0, n, tile, 0)

    return body


def hot_back(counts, line, s, patches):
    live = lax.broadcasted_iota(jnp.int32, (1, SLOTS), 1) < counts[s]
    pick = jnp.where(live, line[s, :, :SLOTS], -1)
    return (lax.broadcasted_iota(jnp.int32, (patches, SLOTS), 0) == pick).astype(f32).astype(bf16)


def mlp_other_body(samples, patches):
    def body(counts, line, c, dm, u0, u1, u2, u3, d0, d1, d2, d3, m, dc, r, gain, out, dr, g2, y, up, down):
        join(counts, samples, (u0, u1, u2, u3), up)
        join(counts, samples, (d0, d1, d2, d3), down)
        n = tiles(total_of(counts, samples))
        g2[...] = jnp.zeros(g2.shape, f32)

        def tile(i, x):
            rr = win(i * TILE)
            cv, dv = c[rr, :], dm[rr, :]
            _, _, mv, dcv = mlp_tile(cv, dv, up, down)
            rv = r[rr, :]
            y[rr, :] = (rv + (m[rr, :] + mv)).astype(bf16)
            dct = dc[rr, :] + dcv
            hat, inv = normed(rv)
            g2[0:1, :] += jnp.sum(dct * hat, axis=0, keepdims=True)
            g2[1:2, :] += jnp.sum(dct, axis=0, keepdims=True)
            dr[rr, :] = dv.astype(f32) + norm_back(dct, hat, inv, gain[...])
            return x

        lax.fori_loop(0, n, tile, 0)
        y[win(n * TILE), :] = jnp.zeros((TILE, y.shape[1]), bf16)

        def scatter(s, start):
            out[s] = dot(hot_back(counts, line, s, patches), y[win(start), :]).astype(bf16)
            return start + ((counts[s] + 15) // 16) * 16

        lax.fori_loop(0, samples, scatter, 0)

    return body


def attend_back(counts, qkv, do, lse, dqkv, samples, width):
    left = lane_halves()
    row = lax.broadcasted_iota(jnp.int32, (SLOTS, 1), 0)

    def one(s, start):
        rows = win(start)
        live = row < counts[s]
        for pair in range(width // 128):
            lo = pair * 128
            q = qkv[rows, lo:lo + 128]
            k = qkv[rows, width + lo:width + lo + 128]
            v = qkv[rows, 2 * width + lo:2 * width + lo + 128]
            dov = do[rows, lo:lo + 128]
            dov = jnp.where(live, dov, jnp.zeros_like(dov))
            zero = jnp.zeros_like(k)
            dq, dk, dvv = [], [], []
            for side in range(2):
                keep = left if side == 0 else ~left
                sc = dot(jnp.where(keep, k, zero), q, NT) * scale
                sc = jnp.where(live, sc, masked_score)
                p = jnp.exp(sc - lse[s, 2 * pair + side:2 * pair + side + 1, :])
                dp = dot(jnp.where(keep, v, zero), dov, NT)
                t = jnp.sum(p * dp, axis=0, keepdims=True)
                ds = (p * (dp - t)).astype(bf16)
                dq.append(dot(ds, k, TN))
                dk.append(dot(ds, q))
                dvv.append(dot(p.astype(bf16), dov))
            dqkv[rows, lo:lo + 128] = (jnp.where(left, dq[0], dq[1]) * scale).astype(bf16)
            dqkv[rows, width + lo:width + lo + 128] = (jnp.where(left, dk[0], dk[1]) * scale).astype(bf16)
            dqkv[rows, 2 * width + lo:2 * width + lo + 128] = jnp.where(left, dvv[0], dvv[1]).astype(bf16)
        return start + ((counts[s] + 15) // 16) * 16

    lax.fori_loop(0, samples, one, 0)


def attn_own_body(samples, width):
    def body(counts, dr, qkv, lse, o, wout, gout, dqkv, do):
        total = total_of(counts, samples)
        n = tiles(total)
        gout[...] = jnp.zeros(gout.shape, f32)

        def first(i, x):
            r = win(i * TILE)
            dz = dr[r, :].astype(bf16)
            do[r, :] = dot(dz, wout[...], NT).astype(bf16)
            gout[...] += dot(o[r, :], dz, TN)
            return x

        lax.fori_loop(0, n, first, 0)
        attend_back(counts, qkv, do, lse, dqkv, samples, width)
        dqkv[win(total), :] = jnp.zeros((TILE, dqkv.shape[1]), bf16)

    return body


def proj_own_body(samples, width):
    def body(counts, dqkv, a, wqkv, da, gqkv):
        n = tiles(total_of(counts, samples))
        gqkv[...] = jnp.zeros(gqkv.shape, f32)

        def last(i, x):
            r = win(i * TILE)
            dv = dqkv[r, :]
            da[r, :] = dot(dv, wqkv[...], NT)
            for j in range(3):
                gqkv[j] += dot(a[r, :], dv[:, j * width:(j + 1) * width], TN)
            return x

        lax.fori_loop(0, n, last, 0)

    return body


def attn_other_body(samples, width):
    def body(counts, dr, qkv, lse, wout, dqkv, do):
        total = total_of(counts, samples)
        n = tiles(total)

        def first(i, x):
            r = win(i * TILE)
            do[r, :] = dot(dr[r, :].astype(bf16), wout[...], NT).astype(bf16)
            return x

        lax.fori_loop(0, n, first, 0)
        attend_back(counts, qkv, do, lse, dqkv, samples, width)
        dqkv[win(total), :] = jnp.zeros((TILE, dqkv.shape[1]), bf16)

    return body


def proj_other_body(samples, patches):
    def body(counts, line, dr, dqkv, wqkv, da, h, gain, out, g1, dh):
        n = tiles(total_of(counts, samples))
        g1[...] = jnp.zeros(g1.shape, f32)

        def last(i, x):
            r = win(i * TILE)
            dat = da[r, :] + dot(dqkv[r, :], wqkv[...], NT)
            hat, inv = normed(h[r, :].astype(f32))
            g1[0:1, :] += jnp.sum(dat * hat, axis=0, keepdims=True)
            g1[1:2, :] += jnp.sum(dat, axis=0, keepdims=True)
            dh[r, :] = (dr[r, :] + norm_back(dat, hat, inv, gain[...])).astype(bf16)
            return x

        lax.fori_loop(0, n, last, 0)
        dh[win(n * TILE), :] = jnp.zeros((TILE, dh.shape[1]), bf16)

        def scatter(s, start):
            out[s] = dot(hot_back(counts, line, s, patches), dh[win(start), :]).astype(bf16)
            return start + ((counts[s] + 15) // 16) * 16

        lax.fori_loop(0, samples, scatter, 0)

    return body


def sds(shape, dtype):
    return jax.ShapeDtypeStruct(shape, dtype)


def call(body, counts, args, outs, scratch=(), flops=0):
    moved = sum(x.size * x.dtype.itemsize for x in list(args) + list(outs))
    return pl.pallas_call(
        body,
        out_shape=list(outs),
        grid_spec=pltpu.PrefetchScalarGridSpec(
            num_scalar_prefetch=1,
            grid=(1,),
            in_specs=[pl.BlockSpec(x.shape, lambda i, n, d=x.ndim: (0,) * d, pipeline_mode=pl.Buffered(1)) for x in args],
            out_specs=[pl.BlockSpec(x.shape, lambda i, n, d=len(x.shape): (0,) * d, pipeline_mode=pl.Buffered(1)) for x in outs],
            scratch_shapes=list(scratch),
        ),
        compiler_params=pltpu.CompilerParams(vmem_limit_bytes=62 << 20),
        cost_estimate=pl.CostEstimate(flops=flops, transcendentals=0, bytes_accessed=moved),
    )(counts, *args)


def fwd_own(counts, col, patches, cot, gain, shift, weight):
    S, L, D = patches.shape
    width = weight.shape[1] // 3
    TP = S * SLOTS + TILE
    whole = lambda d: (lambda s, n: (0,) * d)
    one = lambda s, n: (s, 0, 0)
    B1 = pl.Buffered(1)
    outs = [sds((TP, D), bf16), sds((TP, D), bf16), sds((TP, D), bf16), sds((TP, 3 * width), bf16), sds((TP, width), bf16), sds((S, width // HD, SLOTS), f32)]
    return pl.pallas_call(
        fwd_own_body(S, width),
        name="fwd_own",
        out_shape=outs,
        grid_spec=pltpu.PrefetchScalarGridSpec(
            num_scalar_prefetch=1,
            grid=(S,),
            in_specs=[
                pl.BlockSpec((1, L, 1), one),
                pl.BlockSpec((1, L, D), one),
                pl.BlockSpec((1, L, D), one),
                pl.BlockSpec((1, D), whole(2)),
                pl.BlockSpec((1, D), whole(2)),
                pl.BlockSpec(weight.shape, whole(2), pipeline_mode=B1),
            ],
            out_specs=[pl.BlockSpec(x.shape, whole(len(x.shape)), pipeline_mode=B1) for x in outs],
        ),
        compiler_params=pltpu.CompilerParams(vmem_limit_bytes=62 << 20),
        cost_estimate=pl.CostEstimate(flops=6 * 10**9, transcendentals=0, bytes_accessed=25 << 20),
    )(counts, col, patches, cot, gain, shift, weight)


def fwd_other(counts, a, h, o, wq, out_own, wo, gain, shift, S):
    TP, D = a.shape
    width = wq[0].shape[1] // 3
    outs = [sds((TP, 3 * width), bf16), sds((TP, width), bf16), sds((S, width // HD, SLOTS), f32), sds((TP, D), f32), sds((TP, D), bf16), sds((D, 3 * width), bf16), sds((width, D), bf16)]
    return call(fwd_other_body(S, width), counts, [a, h, o, *wq, *wo, out_own, gain, shift], outs, flops=7 * 10**9)


def mlp_own(counts, c, dm, up, down, S):
    TP, D = c.shape
    outs = [sds((TP, D), f32), sds((TP, D), f32), sds(up.shape, f32), sds(down.shape, f32)]
    return call(mlp_own_body(S), counts, [c, dm, up, down], outs, flops=18 * 10**9)


def mlp_other(counts, line, c, dm, up, down, m, dc, r, gain, S, L):
    TP, D = c.shape
    outs = [sds((S, L, D), bf16), sds((TP, D), f32), sds((8, D), f32)]
    return call(mlp_other_body(S, L), counts, [line, c, dm, *up, *down, m, dc, r, gain], outs, [pltpu.VMEM((TP, D), bf16), pltpu.VMEM((D, 4 * down[0].shape[0]), bf16), pltpu.VMEM((4 * down[0].shape[0], D), bf16)], flops=12 * 10**9)


def attn_own(counts, dr, qkv, lse, o, wout, S):
    TP, width = o.shape
    outs = [sds(wout.shape, f32), sds((TP, 3 * width), bf16)]
    return call(attn_own_body(S, width), counts, [dr, qkv, lse, o, wout], outs, [pltpu.VMEM((TP, width), bf16)], flops=5 * 10**9)


def proj_own(counts, dqkv, a, wqkv, S):
    TP, D = a.shape
    width = wqkv.shape[1] // 3
    outs = [sds((TP, D), f32), sds((3, D, width), f32)]
    return call(proj_own_body(S, width), counts, [dqkv, a, wqkv], outs, flops=5 * 10**9)


def attn_other(counts, dr, qkv, lse, wout, S):
    TP, width = dr.shape[0], wout.shape[0]
    outs = [sds((TP, 3 * width), bf16)]
    return call(attn_other_body(S, width), counts, [dr, qkv, lse, wout], outs, [pltpu.VMEM((TP, width), bf16)], flops=4 * 10**9)[0]


def proj_other(counts, line, dr, dqkv, wqkv, da, h, gain, S, L):
    TP, D = h.shape
    outs = [sds((S, L, D), bf16), sds((8, D), f32)]
    return call(proj_other_body(S, L), counts, [line, dr, dqkv, wqkv, da, h, gain], outs, [pltpu.VMEM((TP, D), bf16)], flops=4 * 10**9)


def swap(x, axis, size, bit):
    return lax.ppermute(x, axis, [(k, k ^ bit) for k in range(size)])


def tie(*xs):
    return lax.optimization_barrier(xs)


def side(bit):
    return (lax.axis_index("dp") // bit) % 2


def half(x, i):
    n = x.shape[0] // 2
    return lax.dynamic_slice_in_dim(x, i * n, n, 0)


def fold(x, bit, dp):
    i = side(bit)
    return half(x, i) + swap(half(x, 1 - i), "dp", dp, bit)


def spread(x, bit, dp):
    got = swap(x, "dp", dp, bit)
    first = side(bit) == 0
    return jnp.where(first, jnp.concatenate([x, got], 0), jnp.concatenate([got, x], 0))


def folds(x, bits, dp):
    for bit in bits:
        x = fold(x, bit, dp)
    return x


def spreads(x, bits, dp):
    for bit in reversed(bits):
        x = spread(x, bit, dp)
    return x


def shards(dp, patches, counts, visible, g1, b1, wq, wo, g2, b2, wu, wd, cot):
    S, L, D = patches.shape
    wt = wq.transpose(1, 0, 2)
    wq = jnp.concatenate([wt[0], wt[1], wt[2]], axis=1)
    col, line = visible[:, :, None], visible[:, None, :]
    g1, b1, g2, b2 = (x[None, :] for x in (g1, b1, g2, b2))
    me = lax.axis_index("dp") % 4
    order = jnp.stack([me, me ^ 2, me ^ 1, me ^ 3]).astype(jnp.int32)

    def part(w):
        rows = w.shape[0] // 4
        return lax.dynamic_slice_in_dim(w, me * rows, rows, 0).astype(f32)

    def rest(first, across):
        return [first, across, swap(first, "dp", dp, 1), swap(across, "dp", dp, 1)]

    counts = jnp.concatenate([counts, order])
    every = [1 << i for i in range(dp.bit_length() - 1)]
    along = every
    other = [1, 4, 2] + every[3:] if len(every) > 2 else every

    fq, fo = swap(part(wq), "tensor", 2, 1), swap(part(wo), "tensor", 2, 1)
    h, dm, a, qkv0, o0, lse0 = fwd_own(counts, col, patches, cot, g1, b1, wq)
    fq, fo, pu, pd, a = tie(fq, fo, part(wu), part(wd), a)
    aq, ao = swap(fq, "dp", dp, 2), swap(fo, "dp", dp, 2)
    fu, fd = swap(pu, "tensor", 2, 1), swap(pd, "tensor", 2, 1)
    wq1, wo1 = rest(fq, aq), rest(fo, ao)
    qkv1, _, lse1, r, c, wq1, wo1 = fwd_other(counts, a, h, o0, wq1, wo, wo1, g2, b2, S)
    fu, fd, c = tie(fu, fd, c)
    au = swap(fu, "dp", dp, 2)
    ad = swap(fd, "dp", dp, 2)
    m, dc, gup, gdown = mlp_own(counts, c, dm, wu, wd, S)
    au, ad, m = tie(au, ad, m)
    wu1, wd1 = rest(fu, au), rest(fd, ad)
    A, B = fold(gup, 1, dp), fold(gdown, 1, dp)
    A, B, c = tie(A, B, c)
    out, dr, gg2 = mlp_other(counts, line, c, dm, wu1, wd1, m, dc, r, g2, S, L)
    A, B = fold(A, along[1], dp), fold(B, other[1], dp)
    A, B, dr = tie(A, B, dr)
    A, B = fold(A, along[2], dp), fold(B, other[2], dp)
    gout, dq0 = attn_own(counts, dr, qkv0, lse0, o0, wo, S)
    A, B, dq0, dr = tie(A, B, dq0, dr)
    A, B, E = folds(A, along[3:], dp), folds(B, other[3:], dp), fold(gout, 1, dp)
    da, gqkv = proj_own(counts, dq0, a, wq, S)
    C = gqkv.reshape(2, (3 * D) // 2, -1)
    C, F = fold(C[0], 1, dp), fold(C[1], 1, dp)
    da, dr = tie(da, dr)
    dq1 = attn_other(counts, dr, qkv1, lse1, wo1, S)
    A, B, C, F, E, dq1 = tie(A, B, C, F, E, dq1)
    A, B = spreads(A, along[3:], dp), spreads(B, other[3:], dp)
    C, F, E = fold(C, along[1], dp), fold(F, other[1], dp), fold(E, other[1], dp)
    gin, gg1 = proj_other(counts, line, dr, dq1, wq1, da, h, g1, S, L)
    C, F, E, A, B, gg1 = tie(C, F, E, A, B, gg1)
    small = jnp.concatenate([gg1, gg2], 0)
    for bit in along[3:]:
        small = small + swap(small, "dp", dp, bit)
    for bit, late in zip(reversed(along[:3]), reversed(other[:3])):
        A, B = spread(A, bit, dp), spread(B, late, dp)
        small = small + swap(small, "dp", dp, bit)
        if bit != 1:
            A, B, small = tie(A, B, small)
    gup, gdown = A, B
    gg1, gg2 = small[:8], small[8:]
    C = spreads(folds(C, along[2:], dp), along, dp)
    F = spreads(folds(F, other[2:], dp), other, dp)
    gqkv = jnp.concatenate([C, F], 0).reshape(3, D, -1)
    gout = spreads(folds(E, other[2:], dp), other, dp)
    return (out, gin, gg1[0], gg1[1], gqkv.transpose(1, 0, 2), gout, gg2[0], gg2[1], gup, gdown)


def solution(mesh):
    dp = mesh.shape["dp"]
    placed = (P("dp", None, None), P("dp"), P("dp", None), P(), P(), P(None, None, "tensor"), P("tensor", None), P(), P(), P(None, "tensor"), P("tensor", None), P("dp", None, None))
    outs = (P("dp", None, None), P("dp", None, None), P(), P(), P(None, None, "tensor"), P("tensor", None), P(), P(), P(None, "tensor"), P("tensor", None))

    def layer(*a):
        return shards(dp, *a)

    return jax.shard_map(layer, mesh=mesh, in_specs=placed, out_specs=outs, check_vma=False)
```

```python
import jax
import jax.numpy as jnp
from jax import lax
from jax.sharding import PartitionSpec as P
from jax.experimental import pallas as pl
from jax.experimental.pallas import tpu as pltpu

HD = 64
SLOTS = 256
TILE = 256
norm_eps = 1e-06
masked_score = -1e30
scale = HD ** (-0.5)
f32, bf16 = jnp.float32, jnp.bfloat16


def dot(x, y, dims=((1,), (0,))):
    return lax.dot_general(x, y, (dims, ((), ())), preferred_element_type=f32)


NT = ((1,), (1,))
TN = ((0,), (0,))


def win(start, size=SLOTS):
    if not isinstance(start, int):
        start = pl.multiple_of(start, 16)
    return pl.ds(start, size)


def start_of(counts, s):
    return lax.fori_loop(0, s, lambda i, t: t + ((counts[i] + 15) // 16) * 16, 0)


def total_of(counts, samples):
    return start_of(counts, samples)


def normed(values):
    center = values - jnp.mean(values, axis=-1, keepdims=True)
    spread = jnp.mean(center * center, axis=-1, keepdims=True)
    inv = lax.rsqrt(spread + norm_eps)
    return center * inv, inv


def norm_back(grad, hat, inv, gain):
    g = grad * gain
    return inv * (g - jnp.mean(g, axis=-1, keepdims=True) - hat * jnp.mean(g * hat, axis=-1, keepdims=True))


def lane_halves():
    lane = lax.broadcasted_iota(jnp.int32, (1, 128), 1)
    return lane < HD


def by_size(counts, s, run):
    few = counts[s] <= SLOTS // 2

    @pl.when(few)
    def _():
        run(SLOTS // 2)

    @pl.when(jnp.logical_not(few))
    def _():
        run(SLOTS)


def lanes(start):
    return pl.ds(pl.multiple_of(start, 128), 128)


def attend_rows(counts, qkv, out, lse, samples, width):
    left = lane_halves()

    def one(s, start):
        def run(size):
            rows = win(start, size)
            live = lax.broadcasted_iota(jnp.int32, (size, 1), 0) < counts[s]

            def pair(j, x):
                lo = j * 128
                q = qkv[rows, lanes(lo)]
                k = qkv[rows, lanes(width + lo)]
                v = qkv[rows, lanes(2 * width + lo)]
                parts = []
                for side in range(2):
                    keep = left if side == 0 else ~left
                    sc = dot(jnp.where(keep, k, jnp.zeros_like(k)), q, NT) * scale
                    sc = jnp.where(live, sc, masked_score)
                    top = jnp.max(sc, axis=0, keepdims=True)
                    w = jnp.exp(sc - top)
                    tot = jnp.sum(w, axis=0, keepdims=True)
                    lse[s, j, side:side + 1, :size] = top + jnp.log(tot)
                    p = (w * (1.0 / tot)).astype(bf16)
                    parts.append(dot(p, v, TN))
                out[rows, lanes(lo)] = jnp.where(left, parts[0], parts[1]).astype(bf16)
                return x

            lax.fori_loop(0, width // 128, pair, 0)

        by_size(counts, s, run)
        return start + ((counts[s] + 15) // 16) * 16

    lax.fori_loop(0, samples, one, 0)


def tiles(total):
    return (total + TILE - 1) // TILE


def fwd_own_body(samples, width):
    def body(counts, col, patches, cot, gain, shift, weight, h, dm, a, qkv, o, lse):
        s = pl.program_id(0)
        start = start_of(counts, s)
        pick = col[0, :SLOTS, :]
        row = lax.broadcasted_iota(jnp.int32, (SLOTS, 1), 0)
        pick = jnp.where(row < counts[s], pick, -1)
        hot = (lax.broadcasted_iota(jnp.int32, (SLOTS, patches.shape[1]), 1) == pick).astype(f32).astype(bf16)
        h[win(start), :] = dot(hot, patches[0]).astype(bf16)
        dm[win(start), :] = dot(hot, cot[0]).astype(bf16)

        @pl.when(s == samples - 1)
        def _():
            total = total_of(counts, samples)
            zeros = jnp.zeros((TILE, h.shape[1]), bf16)
            h[win(total), :] = zeros
            dm[win(total), :] = zeros

            def tile(i, c):
                r = win(i * TILE)
                hat, _ = normed(h[r, :].astype(f32))
                av = (hat * gain[...] + shift[...]).astype(bf16)
                a[r, :] = av
                qkv[r, :] = dot(av, weight[...]).astype(bf16)
                return c

            n = tiles(total)
            lax.fori_loop(0, n, tile, 0)
            qkv[win(n * TILE), :] = jnp.zeros((TILE, qkv.shape[1]), bf16)
            attend_rows(counts, qkv, o, lse, samples, width)
            o[win(total), :] = jnp.zeros((TILE, width), bf16)

    return body


def join(counts, samples, pieces, full):
    rows = pieces[0].shape[0]
    for i in range(4):
        full[pl.ds(pl.multiple_of(counts[samples + i] * rows, 16), rows), :] = pieces[i][...].astype(bf16)


def fwd_other_body(samples, width):
    def body(counts, a, h, o, q0, q1, q2, q3, w0, w1, w2, w3, out_own, gain, shift, qkv, o2, lse, r, c, weight, out_other):
        join(counts, samples, (q0, q1, q2, q3), weight)
        join(counts, samples, (w0, w1, w2, w3), out_other)
        total = total_of(counts, samples)
        n = tiles(total)

        def tile(i, x):
            rr = win(i * TILE)
            qkv[rr, :] = dot(a[rr, :], weight[...]).astype(bf16)
            return x

        lax.fori_loop(0, n, tile, 0)
        qkv[win(n * TILE), :] = jnp.zeros((TILE, qkv.shape[1]), bf16)
        attend_rows(counts, qkv, o2, lse, samples, width)
        o2[win(total), :] = jnp.zeros((TILE, width), bf16)

        def tail(i, x):
            rr = win(i * TILE)
            z = dot(o[rr, :], out_own[...]) + dot(o2[rr, :], out_other[...])
            rv = h[rr, :].astype(f32) + z
            r[rr, :] = rv
            hat, _ = normed(rv)
            c[rr, :] = (hat * gain[...] + shift[...]).astype(bf16)
            return x

        lax.fori_loop(0, n, tail, 0)

    return body


def gelu_both(u):
    cdf = 0.5 * (1.0 + lax.erf(u * (0.5 ** 0.5)))
    pdf = jnp.exp(-0.5 * u * u) * (0.5 / jnp.pi) ** 0.5
    return u * cdf, cdf + u * pdf


def mlp_tile(cv, dv, up, down):
    u = dot(cv, up[...])
    e, slope = gelu_both(u)
    e = e.astype(bf16)
    m = dot(e, down[...])
    de = dot(dv, down[...], NT)
    du = (de * slope).astype(bf16)
    dc = dot(du, up[...], NT)
    return e, du, m, dc


def mlp_own_body(samples):
    def body(counts, c, dm, up, down, m, dc, gup, gdown):
        n = tiles(total_of(counts, samples))
        gup[...] = jnp.zeros(gup.shape, f32)
        gdown[...] = jnp.zeros(gdown.shape, f32)

        def tile(i, x):
            r = win(i * TILE)
            cv, dv = c[r, :], dm[r, :]
            e, du, mv, dcv = mlp_tile(cv, dv, up, down)
            m[r, :] = mv
            dc[r, :] = dcv
            gdown[...] += dot(e, dv, TN)
            gup[...] += dot(cv, du, TN)
            return x

        lax.fori_loop(0, n, tile, 0)

    return body


def hot_back(counts, line, s, patches):
    live = lax.broadcasted_iota(jnp.int32, (1, SLOTS), 1) < counts[s]
    pick = jnp.where(live, line[s, :, :SLOTS], -1)
    return (lax.broadcasted_iota(jnp.int32, (patches, SLOTS), 0) == pick).astype(f32).astype(bf16)


def mlp_other_body(samples, patches):
    def body(counts, line, c, dm, u0, u1, u2, u3, d0, d1, d2, d3, m, dc, r, gain, out, dr, g2, y, up, down):
        join(counts, samples, (u0, u1, u2, u3), up)
        join(counts, samples, (d0, d1, d2, d3), down)
        n = tiles(total_of(counts, samples))
        g2[...] = jnp.zeros(g2.shape, f32)

        def tile(i, x):
            rr = win(i * TILE)
            cv, dv = c[rr, :], dm[rr, :]
            _, _, mv, dcv = mlp_tile(cv, dv, up, down)
            rv = r[rr, :]
            y[rr, :] = (rv + (m[rr, :] + mv)).astype(bf16)
            dct = dc[rr, :] + dcv
            hat, inv = normed(rv)
            g2[0:1, :] += jnp.sum(dct * hat, axis=0, keepdims=True)
            g2[1:2, :] += jnp.sum(dct, axis=0, keepdims=True)
            dr[rr, :] = dv.astype(f32) + norm_back(dct, hat, inv, gain[...])
            return x

        lax.fori_loop(0, n, tile, 0)
        y[win(n * TILE), :] = jnp.zeros((TILE, y.shape[1]), bf16)

        def scatter(s, start):
            out[s] = dot(hot_back(counts, line, s, patches), y[win(start), :]).astype(bf16)
            return start + ((counts[s] + 15) // 16) * 16

        lax.fori_loop(0, samples, scatter, 0)

    return body


def attend_back(counts, qkv, do, lse, dqkv, samples, width):
    left = lane_halves()

    def one(s, start):
        def run(size):
            rows = win(start, size)
            live = lax.broadcasted_iota(jnp.int32, (size, 1), 0) < counts[s]

            def pair(j, x):
                lo = j * 128
                q = qkv[rows, lanes(lo)]
                k = qkv[rows, lanes(width + lo)]
                v = qkv[rows, lanes(2 * width + lo)]
                dov = do[rows, lanes(lo)]
                dov = jnp.where(live, dov, jnp.zeros_like(dov))
                zero = jnp.zeros_like(k)
                dq, dk, dvv = [], [], []
                for side in range(2):
                    keep = left if side == 0 else ~left
                    sc = dot(jnp.where(keep, k, zero), q, NT) * scale
                    sc = jnp.where(live, sc, masked_score)
                    p = jnp.exp(sc - lse[s, j, side:side + 1, :size])
                    dp = dot(jnp.where(keep, v, zero), dov, NT)
                    t = jnp.sum(p * dp, axis=0, keepdims=True)
                    ds = (p * (dp - t)).astype(bf16)
                    dq.append(dot(ds, k, TN))
                    dk.append(dot(ds, q))
                    dvv.append(dot(p.astype(bf16), dov))
                dqkv[rows, lanes(lo)] = (jnp.where(left, dq[0], dq[1]) * scale).astype(bf16)
                dqkv[rows, lanes(width + lo)] = (jnp.where(left, dk[0], dk[1]) * scale).astype(bf16)
                dqkv[rows, lanes(2 * width + lo)] = jnp.where(left, dvv[0], dvv[1]).astype(bf16)
                return x

            lax.fori_loop(0, width // 128, pair, 0)

        by_size(counts, s, run)
        return start + ((counts[s] + 15) // 16) * 16

    lax.fori_loop(0, samples, one, 0)


def attn_own_body(samples, width):
    def body(counts, dr, qkv, lse, o, wout, gout, dqkv, do):
        total = total_of(counts, samples)
        n = tiles(total)
        gout[...] = jnp.zeros(gout.shape, f32)

        def first(i, x):
            r = win(i * TILE)
            dz = dr[r, :].astype(bf16)
            do[r, :] = dot(dz, wout[...], NT).astype(bf16)
            gout[...] += dot(o[r, :], dz, TN)
            return x

        lax.fori_loop(0, n, first, 0)
        attend_back(counts, qkv, do, lse, dqkv, samples, width)
        dqkv[win(total), :] = jnp.zeros((TILE, dqkv.shape[1]), bf16)

    return body


def proj_own_body(samples, width):
    def body(counts, dqkv, a, wqkv, da, gqkv):
        n = tiles(total_of(counts, samples))
        gqkv[...] = jnp.zeros(gqkv.shape, f32)

        def last(i, x):
            r = win(i * TILE)
            dv = dqkv[r, :]
            da[r, :] = dot(dv, wqkv[...], NT)
            for j in range(3):
                gqkv[j] += dot(a[r, :], dv[:, j * width:(j + 1) * width], TN)
            return x

        lax.fori_loop(0, n, last, 0)

    return body


def attn_other_body(samples, width):
    def body(counts, dr, qkv, lse, wout, dqkv, do):
        total = total_of(counts, samples)
        n = tiles(total)

        def first(i, x):
            r = win(i * TILE)
            do[r, :] = dot(dr[r, :].astype(bf16), wout[...], NT).astype(bf16)
            return x

        lax.fori_loop(0, n, first, 0)
        attend_back(counts, qkv, do, lse, dqkv, samples, width)
        dqkv[win(total), :] = jnp.zeros((TILE, dqkv.shape[1]), bf16)

    return body


def proj_other_body(samples, patches):
    def body(counts, line, dr, dqkv, wqkv, da, h, gain, out, g1, dh):
        n = tiles(total_of(counts, samples))
        g1[...] = jnp.zeros(g1.shape, f32)

        def last(i, x):
            r = win(i * TILE)
            dat = da[r, :] + dot(dqkv[r, :], wqkv[...], NT)
            hat, inv = normed(h[r, :].astype(f32))
            g1[0:1, :] += jnp.sum(dat * hat, axis=0, keepdims=True)
            g1[1:2, :] += jnp.sum(dat, axis=0, keepdims=True)
            dh[r, :] = (dr[r, :] + norm_back(dat, hat, inv, gain[...])).astype(bf16)
            return x

        lax.fori_loop(0, n, last, 0)
        dh[win(n * TILE), :] = jnp.zeros((TILE, dh.shape[1]), bf16)

        def scatter(s, start):
            out[s] = dot(hot_back(counts, line, s, patches), dh[win(start), :]).astype(bf16)
            return start + ((counts[s] + 15) // 16) * 16

        lax.fori_loop(0, samples, scatter, 0)

    return body


def sds(shape, dtype):
    return jax.ShapeDtypeStruct(shape, dtype)


def call(body, counts, args, outs, scratch=(), flops=0):
    moved = sum(x.size * x.dtype.itemsize for x in list(args) + list(outs))
    return pl.pallas_call(
        body,
        out_shape=list(outs),
        grid_spec=pltpu.PrefetchScalarGridSpec(
            num_scalar_prefetch=1,
            grid=(1,),
            in_specs=[pl.BlockSpec(x.shape, lambda i, n, d=x.ndim: (0,) * d, pipeline_mode=pl.Buffered(1)) for x in args],
            out_specs=[pl.BlockSpec(x.shape, lambda i, n, d=len(x.shape): (0,) * d, pipeline_mode=pl.Buffered(1)) for x in outs],
            scratch_shapes=list(scratch),
        ),
        compiler_params=pltpu.CompilerParams(vmem_limit_bytes=62 << 20),
        cost_estimate=pl.CostEstimate(flops=flops, transcendentals=0, bytes_accessed=moved),
    )(counts, *args)


def fwd_own(counts, col, patches, cot, gain, shift, weight):
    S, L, D = patches.shape
    width = weight.shape[1] // 3
    TP = S * SLOTS + TILE
    whole = lambda d: (lambda s, n: (0,) * d)
    one = lambda s, n: (s, 0, 0)
    B1 = pl.Buffered(1)
    outs = [sds((TP, D), bf16), sds((TP, D), bf16), sds((TP, D), bf16), sds((TP, 3 * width), bf16), sds((TP, width), bf16), sds((S, width // 128, 2, SLOTS), f32)]
    return pl.pallas_call(
        fwd_own_body(S, width),
        name="fwd_own",
        out_shape=outs,
        grid_spec=pltpu.PrefetchScalarGridSpec(
            num_scalar_prefetch=1,
            grid=(S,),
            in_specs=[
                pl.BlockSpec((1, L, 1), one),
                pl.BlockSpec((1, L, D), one),
                pl.BlockSpec((1, L, D), one),
                pl.BlockSpec((1, D), whole(2)),
                pl.BlockSpec((1, D), whole(2)),
                pl.BlockSpec(weight.shape, whole(2), pipeline_mode=B1),
            ],
            out_specs=[pl.BlockSpec(x.shape, whole(len(x.shape)), pipeline_mode=B1) for x in outs],
        ),
        compiler_params=pltpu.CompilerParams(vmem_limit_bytes=62 << 20),
        cost_estimate=pl.CostEstimate(flops=6 * 10**9, transcendentals=0, bytes_accessed=25 << 20),
    )(counts, col, patches, cot, gain, shift, weight)


def fwd_other(counts, a, h, o, wq, out_own, wo, gain, shift, S):
    TP, D = a.shape
    width = wq[0].shape[1] // 3
    outs = [sds((TP, 3 * width), bf16), sds((TP, width), bf16), sds((S, width // 128, 2, SLOTS), f32), sds((TP, D), f32), sds((TP, D), bf16), sds((D, 3 * width), bf16), sds((width, D), bf16)]
    return call(fwd_other_body(S, width), counts, [a, h, o, *wq, *wo, out_own, gain, shift], outs, flops=7 * 10**9)


def mlp_own(counts, c, dm, up, down, S):
    TP, D = c.shape
    outs = [sds((TP, D), f32), sds((TP, D), f32), sds(up.shape, f32), sds(down.shape, f32)]
    return call(mlp_own_body(S), counts, [c, dm, up, down], outs, flops=18 * 10**9)


def mlp_other(counts, line, c, dm, up, down, m, dc, r, gain, S, L):
    TP, D = c.shape
    outs = [sds((S, L, D), bf16), sds((TP, D), f32), sds((8, D), f32)]
    return call(mlp_other_body(S, L), counts, [line, c, dm, *up, *down, m, dc, r, gain], outs, [pltpu.VMEM((TP, D), bf16), pltpu.VMEM((D, 4 * down[0].shape[0]), bf16), pltpu.VMEM((4 * down[0].shape[0], D), bf16)], flops=12 * 10**9)


def attn_own(counts, dr, qkv, lse, o, wout, S):
    TP, width = o.shape
    outs = [sds(wout.shape, f32), sds((TP, 3 * width), bf16)]
    return call(attn_own_body(S, width), counts, [dr, qkv, lse, o, wout], outs, [pltpu.VMEM((TP, width), bf16)], flops=5 * 10**9)


def proj_own(counts, dqkv, a, wqkv, S):
    TP, D = a.shape
    width = wqkv.shape[1] // 3
    outs = [sds((TP, D), f32), sds((3, D, width), f32)]
    return call(proj_own_body(S, width), counts, [dqkv, a, wqkv], outs, flops=5 * 10**9)


def attn_other(counts, dr, qkv, lse, wout, S):
    TP, width = dr.shape[0], wout.shape[0]
    outs = [sds((TP, 3 * width), bf16)]
    return call(attn_other_body(S, width), counts, [dr, qkv, lse, wout], outs, [pltpu.VMEM((TP, width), bf16)], flops=4 * 10**9)[0]


def proj_other(counts, line, dr, dqkv, wqkv, da, h, gain, S, L):
    TP, D = h.shape
    outs = [sds((S, L, D), bf16), sds((8, D), f32)]
    return call(proj_other_body(S, L), counts, [line, dr, dqkv, wqkv, da, h, gain], outs, [pltpu.VMEM((TP, D), bf16)], flops=4 * 10**9)


def swap(x, axis, size, bit):
    return lax.ppermute(x, axis, [(k, k ^ bit) for k in range(size)])


def tie(*xs):
    return lax.optimization_barrier(xs)


def side(bit):
    return (lax.axis_index("dp") // bit) % 2


def half(x, i):
    n = x.shape[0] // 2
    return lax.dynamic_slice_in_dim(x, i * n, n, 0)


def fold(x, bit, dp):
    i = side(bit)
    return half(x, i) + swap(half(x, 1 - i), "dp", dp, bit)


def spread(x, bit, dp):
    got = swap(x, "dp", dp, bit)
    first = side(bit) == 0
    return jnp.where(first, jnp.concatenate([x, got], 0), jnp.concatenate([got, x], 0))


def folds(x, bits, dp):
    for bit in bits:
        x = fold(x, bit, dp)
    return x


def spreads(x, bits, dp):
    for bit in reversed(bits):
        x = spread(x, bit, dp)
    return x


def shards(dp, patches, counts, visible, g1, b1, wq, wo, g2, b2, wu, wd, cot):
    S, L, D = patches.shape
    wt = wq.transpose(1, 0, 2)
    wq = jnp.concatenate([wt[0], wt[1], wt[2]], axis=1)
    col, line = visible[:, :, None], visible[:, None, :]
    g1, b1, g2, b2 = (x[None, :] for x in (g1, b1, g2, b2))
    me = lax.axis_index("dp") % 4
    order = jnp.stack([me, me ^ 2, me ^ 1, me ^ 3]).astype(jnp.int32)

    def part(w):
        rows = w.shape[0] // 4
        return lax.dynamic_slice_in_dim(w, me * rows, rows, 0).astype(f32)

    def rest(first, across):
        return [first, across, swap(first, "dp", dp, 1), swap(across, "dp", dp, 1)]

    counts = jnp.concatenate([counts, order])
    every = [1 << i for i in range(dp.bit_length() - 1)]
    along = every
    other = [1, 4, 2] + every[3:] if len(every) > 2 else every

    fq, fo = swap(part(wq), "tensor", 2, 1), swap(part(wo), "tensor", 2, 1)
    h, dm, a, qkv0, o0, lse0 = fwd_own(counts, col, patches, cot, g1, b1, wq)
    fq, fo, pu, pd, a = tie(fq, fo, part(wu), part(wd), a)
    aq = swap(fq, "dp", dp, 2)
    ao = swap(fo, "dp", dp, 2)
    fu = swap(pu, "tensor", 2, 1)
    fd = swap(pd, "tensor", 2, 1)
    wq1, wo1 = rest(fq, aq), rest(fo, ao)
    qkv1, _, lse1, r, c, wq1, wo1 = fwd_other(counts, a, h, o0, wq1, wo, wo1, g2, b2, S)
    fu, fd, c = tie(fu, fd, c)
    au = swap(fu, "dp", dp, 2)
    ad = swap(fd, "dp", dp, 2)
    m, dc, gup, gdown = mlp_own(counts, c, dm, wu, wd, S)
    au, ad, m = tie(au, ad, m)
    wu1, wd1 = rest(fu, au), rest(fd, ad)
    A, B = fold(gup, 1, dp), fold(gdown, 1, dp)
    A, B, c = tie(A, B, c)
    out, dr, gg2 = mlp_other(counts, line, c, dm, wu1, wd1, m, dc, r, g2, S, L)
    A, B = fold(A, along[1], dp), fold(B, other[1], dp)
    A, B, dr = tie(A, B, dr)
    A, B = fold(A, along[2], dp), fold(B, other[2], dp)
    gout, dq0 = attn_own(counts, dr, qkv0, lse0, o0, wo, S)
    A, B, dq0, dr = tie(A, B, dq0, dr)
    A, B, E = folds(A, along[3:], dp), folds(B, other[3:], dp), fold(gout, 1, dp)
    da, gqkv = proj_own(counts, dq0, a, wq, S)
    C = gqkv.reshape(2, (3 * D) // 2, -1)
    C, F = fold(C[0], 1, dp), fold(C[1], 1, dp)
    da, dr = tie(da, dr)
    dq1 = attn_other(counts, dr, qkv1, lse1, wo1, S)
    A, B, C, F, E, dq1 = tie(A, B, C, F, E, dq1)
    A, B = spreads(A, along[3:], dp), spreads(B, other[3:], dp)
    C, F, E = fold(C, along[1], dp), fold(F, other[1], dp), fold(E, other[1], dp)
    gin, gg1 = proj_other(counts, line, dr, dq1, wq1, da, h, g1, S, L)
    C, F, E, A, B, gg1 = tie(C, F, E, A, B, gg1)
    small = jnp.concatenate([gg1, gg2], 0)
    for bit in along[3:]:
        small = small + swap(small, "dp", dp, bit)
    for bit, late in zip(reversed(along[:3]), reversed(other[:3])):
        A, B = spread(A, bit, dp), spread(B, late, dp)
        small = small + swap(small, "dp", dp, bit)
        if bit != 1:
            A, B, small = tie(A, B, small)
    gup, gdown = A, B
    gg1, gg2 = small[:8], small[8:]
    C = spreads(folds(C, along[2:], dp), along, dp)
    F = spreads(folds(F, other[2:], dp), other, dp)
    gqkv = jnp.concatenate([C, F], 0).reshape(3, D, -1)
    gout = spreads(folds(E, other[2:], dp), other, dp)
    return (out, gin, gg1[0], gg1[1], gqkv.transpose(1, 0, 2), gout, gg2[0], gg2[1], gup, gdown)


def solution(mesh):
    dp = mesh.shape["dp"]
    placed = (P("dp", None, None), P("dp"), P("dp", None), P(), P(), P(None, None, "tensor"), P("tensor", None), P(), P(), P(None, "tensor"), P("tensor", None), P("dp", None, None))
    outs = (P("dp", None, None), P("dp", None, None), P(), P(), P(None, None, "tensor"), P("tensor", None), P(), P(), P(None, "tensor"), P("tensor", None))

    def layer(*a):
        return shards(dp, *a)

    return jax.shard_map(layer, mesh=mesh, in_specs=placed, out_specs=outs, check_vma=False)
```

```python
import jax
import jax.numpy as jnp
from jax import lax
from jax.sharding import PartitionSpec as P
from jax.experimental import pallas as pl
from jax.experimental.pallas import tpu as pltpu

HD = 64
SLOTS = 256
TILE = 256
norm_eps = 1e-06
masked_score = -1e30
scale = HD ** (-0.5)
f32, bf16 = jnp.float32, jnp.bfloat16


def dot(x, y, dims=((1,), (0,))):
    return lax.dot_general(x, y, (dims, ((), ())), preferred_element_type=f32)


NT = ((1,), (1,))
TN = ((0,), (0,))


def win(start, size=SLOTS):
    if not isinstance(start, int):
        start = pl.multiple_of(start, 16)
    return pl.ds(start, size)


def start_of(counts, s):
    return lax.fori_loop(0, s, lambda i, t: t + ((counts[i] + 15) // 16) * 16, 0)


def total_of(counts, samples):
    return start_of(counts, samples)


def normed(values):
    center = values - jnp.mean(values, axis=-1, keepdims=True)
    spread = jnp.mean(center * center, axis=-1, keepdims=True)
    inv = lax.rsqrt(spread + norm_eps)
    return center * inv, inv


def norm_back(grad, hat, inv, gain):
    g = grad * gain
    return inv * (g - jnp.mean(g, axis=-1, keepdims=True) - hat * jnp.mean(g * hat, axis=-1, keepdims=True))


def lane_halves():
    lane = lax.broadcasted_iota(jnp.int32, (1, 128), 1)
    return lane < HD


def by_size(counts, s, run):
    few = counts[s] <= SLOTS // 2

    @pl.when(few)
    def _():
        run(SLOTS // 2)

    @pl.when(jnp.logical_not(few))
    def _():
        run(SLOTS)


def lanes(start):
    return slice(start, start + 128)


def attend_rows(counts, qkv, out, lse, samples, width):
    left = lane_halves()

    def one(s, start):
        def run(size):
            rows = win(start, size)
            live = lax.broadcasted_iota(jnp.int32, (size, 1), 0) < counts[s]

            def pair(j, x):
                lo = j * 128
                q = qkv[rows, lanes(lo)]
                k = qkv[rows, lanes(width + lo)]
                v = qkv[rows, lanes(2 * width + lo)]
                parts = []
                for side in range(2):
                    keep = left if side == 0 else ~left
                    sc = dot(jnp.where(keep, k, jnp.zeros_like(k)), q, NT) * scale
                    sc = jnp.where(live, sc, masked_score)
                    top = jnp.max(sc, axis=0, keepdims=True)
                    w = jnp.exp(sc - top)
                    tot = jnp.sum(w, axis=0, keepdims=True)
                    lse[s, j, side:side + 1, :size] = top + jnp.log(tot)
                    if size < SLOTS:
                        lse[s, j, side:side + 1, size:] = jnp.full((1, SLOTS - size), 1e30, f32)
                    p = (w * (1.0 / tot)).astype(bf16)
                    parts.append(dot(p, v, TN))
                out[rows, lanes(lo)] = jnp.where(left, parts[0], parts[1]).astype(bf16)
                return x

            for j in range(width // 128):
                pair(j, 0)

        by_size(counts, s, run)
        return start + ((counts[s] + 15) // 16) * 16

    lax.fori_loop(0, samples, one, 0)


def tiles(total):
    return (total + TILE - 1) // TILE


def fwd_own_body(samples, width):
    def body(counts, col, patches, cot, gain, shift, weight, h, dm, a, qkv, o, lse):
        s = pl.program_id(0)
        start = start_of(counts, s)
        pick = col[0, :SLOTS, :]
        row = lax.broadcasted_iota(jnp.int32, (SLOTS, 1), 0)
        pick = jnp.where(row < counts[s], pick, -1)
        hot = (lax.broadcasted_iota(jnp.int32, (SLOTS, patches.shape[1]), 1) == pick).astype(f32).astype(bf16)
        h[win(start), :] = dot(hot, patches[0]).astype(bf16)
        dm[win(start), :] = dot(hot, cot[0]).astype(bf16)

        @pl.when(s == samples - 1)
        def _():
            total = total_of(counts, samples)
            zeros = jnp.zeros((TILE, h.shape[1]), bf16)
            h[win(total), :] = zeros
            dm[win(total), :] = zeros

            def tile(i, c):
                r = win(i * TILE)
                hat, _ = normed(h[r, :].astype(f32))
                av = (hat * gain[...] + shift[...]).astype(bf16)
                a[r, :] = av
                qkv[r, :] = dot(av, weight[...]).astype(bf16)
                return c

            n = tiles(total)
            lax.fori_loop(0, n, tile, 0)
            qkv[win(n * TILE), :] = jnp.zeros((TILE, qkv.shape[1]), bf16)
            attend_rows(counts, qkv, o, lse, samples, width)
            o[win(total), :] = jnp.zeros((TILE, width), bf16)

    return body


def join(counts, samples, pieces, full):
    rows = pieces[0].shape[0]
    for i in range(4):
        full[pl.ds(pl.multiple_of(counts[samples + i] * rows, 16), rows), :] = pieces[i][...].astype(bf16)


def fwd_other_body(samples, width):
    def body(counts, a, h, o, q0, q1, q2, q3, w0, w1, w2, w3, out_own, gain, shift, qkv, o2, lse, r, c, weight, out_other):
        join(counts, samples, (q0, q1, q2, q3), weight)
        join(counts, samples, (w0, w1, w2, w3), out_other)
        total = total_of(counts, samples)
        n = tiles(total)

        def tile(i, x):
            rr = win(i * TILE)
            qkv[rr, :] = dot(a[rr, :], weight[...]).astype(bf16)
            return x

        lax.fori_loop(0, n, tile, 0)
        qkv[win(n * TILE), :] = jnp.zeros((TILE, qkv.shape[1]), bf16)
        attend_rows(counts, qkv, o2, lse, samples, width)
        o2[win(total), :] = jnp.zeros((TILE, width), bf16)

        def tail(i, x):
            rr = win(i * TILE)
            z = dot(o[rr, :], out_own[...]) + dot(o2[rr, :], out_other[...])
            rv = h[rr, :].astype(f32) + z
            r[rr, :] = rv
            hat, _ = normed(rv)
            c[rr, :] = (hat * gain[...] + shift[...]).astype(bf16)
            return x

        lax.fori_loop(0, n, tail, 0)

    return body


def gelu_both(u):
    cdf = 0.5 * (1.0 + lax.erf(u * (0.5 ** 0.5)))
    pdf = jnp.exp(-0.5 * u * u) * (0.5 / jnp.pi) ** 0.5
    return u * cdf, cdf + u * pdf


def mlp_tile(cv, dv, up, down):
    u = dot(cv, up[...])
    e, slope = gelu_both(u)
    e = e.astype(bf16)
    m = dot(e, down[...])
    de = dot(dv, down[...], NT)
    du = (de * slope).astype(bf16)
    dc = dot(du, up[...], NT)
    return e, du, m, dc


def mlp_own_body(samples):
    def body(counts, c, dm, up, down, m, dc, gup, gdown):
        n = tiles(total_of(counts, samples))
        gup[...] = jnp.zeros(gup.shape, f32)
        gdown[...] = jnp.zeros(gdown.shape, f32)

        def tile(i, x):
            r = win(i * TILE)
            cv, dv = c[r, :], dm[r, :]
            e, du, mv, dcv = mlp_tile(cv, dv, up, down)
            m[r, :] = mv
            dc[r, :] = dcv
            gdown[...] += dot(e, dv, TN)
            gup[...] += dot(cv, du, TN)
            return x

        lax.fori_loop(0, n, tile, 0)

    return body


def hot_back(counts, line, s, patches):
    live = lax.broadcasted_iota(jnp.int32, (1, SLOTS), 1) < counts[s]
    pick = jnp.where(live, line[s, :, :SLOTS], -1)
    return (lax.broadcasted_iota(jnp.int32, (patches, SLOTS), 0) == pick).astype(f32).astype(bf16)


def mlp_other_body(samples, patches):
    def body(counts, line, c, dm, u0, u1, u2, u3, d0, d1, d2, d3, m, dc, r, gain, out, dr, g2, y, up, down):
        join(counts, samples, (u0, u1, u2, u3), up)
        join(counts, samples, (d0, d1, d2, d3), down)
        n = tiles(total_of(counts, samples))
        g2[...] = jnp.zeros(g2.shape, f32)

        def tile(i, x):
            rr = win(i * TILE)
            cv, dv = c[rr, :], dm[rr, :]
            _, _, mv, dcv = mlp_tile(cv, dv, up, down)
            rv = r[rr, :]
            y[rr, :] = (rv + (m[rr, :] + mv)).astype(bf16)
            dct = dc[rr, :] + dcv
            hat, inv = normed(rv)
            g2[0:1, :] += jnp.sum(dct * hat, axis=0, keepdims=True)
            g2[1:2, :] += jnp.sum(dct, axis=0, keepdims=True)
            dr[rr, :] = dv.astype(f32) + norm_back(dct, hat, inv, gain[...])
            return x

        lax.fori_loop(0, n, tile, 0)
        y[win(n * TILE), :] = jnp.zeros((TILE, y.shape[1]), bf16)

        def scatter(s, start):
            out[s] = dot(hot_back(counts, line, s, patches), y[win(start), :]).astype(bf16)
            return start + ((counts[s] + 15) // 16) * 16

        lax.fori_loop(0, samples, scatter, 0)

    return body


def attend_back(counts, qkv, do, lse, dqkv, samples, width):
    left = lane_halves()

    def one(s, start):
        def run(size):
            rows = win(start, size)
            live = lax.broadcasted_iota(jnp.int32, (size, 1), 0) < counts[s]

            def pair(j, x):
                lo = j * 128
                q = qkv[rows, lanes(lo)]
                k = qkv[rows, lanes(width + lo)]
                v = qkv[rows, lanes(2 * width + lo)]
                dov = do[rows, lanes(lo)]
                dov = jnp.where(live, dov, jnp.zeros_like(dov))
                zero = jnp.zeros_like(k)
                dq, dk, dvv = [], [], []
                for side in range(2):
                    keep = left if side == 0 else ~left
                    sc = dot(jnp.where(keep, k, zero), q, NT) * scale
                    sc = jnp.where(live, sc, masked_score)
                    p = jnp.exp(sc - lse[s, j, side:side + 1, :size])
                    dp = dot(jnp.where(keep, v, zero), dov, NT)
                    t = jnp.sum(p * dp, axis=0, keepdims=True)
                    ds = (p * (dp - t)).astype(bf16)
                    dq.append(dot(ds, k, TN))
                    dk.append(dot(ds, q))
                    dvv.append(dot(p.astype(bf16), dov))
                dqkv[rows, lanes(lo)] = (jnp.where(left, dq[0], dq[1]) * scale).astype(bf16)
                dqkv[rows, lanes(width + lo)] = (jnp.where(left, dk[0], dk[1]) * scale).astype(bf16)
                dqkv[rows, lanes(2 * width + lo)] = jnp.where(left, dvv[0], dvv[1]).astype(bf16)
                return x

            for j in range(width // 128):
                pair(j, 0)

        run(SLOTS)
        return start + ((counts[s] + 15) // 16) * 16

    lax.fori_loop(0, samples, one, 0)


def attn_own_body(samples, width):
    def body(counts, dr, qkv, lse, o, wout, gout, dqkv, do):
        total = total_of(counts, samples)
        n = tiles(total)
        gout[...] = jnp.zeros(gout.shape, f32)

        def first(i, x):
            r = win(i * TILE)
            dz = dr[r, :].astype(bf16)
            do[r, :] = dot(dz, wout[...], NT).astype(bf16)
            gout[...] += dot(o[r, :], dz, TN)
            return x

        lax.fori_loop(0, n, first, 0)
        attend_back(counts, qkv, do, lse, dqkv, samples, width)
        dqkv[win(total), :] = jnp.zeros((TILE, dqkv.shape[1]), bf16)

    return body


def proj_own_body(samples, width):
    def body(counts, dqkv, a, wqkv, da, gqkv):
        n = tiles(total_of(counts, samples))
        gqkv[...] = jnp.zeros(gqkv.shape, f32)

        def last(i, x):
            r = win(i * TILE)
            dv = dqkv[r, :]
            da[r, :] = dot(dv, wqkv[...], NT)
            for j in range(3):
                gqkv[j] += dot(a[r, :], dv[:, j * width:(j + 1) * width], TN)
            return x

        lax.fori_loop(0, n, last, 0)

    return body


def attn_other_body(samples, width):
    def body(counts, dr, qkv, lse, wout, dqkv, do):
        total = total_of(counts, samples)
        n = tiles(total)

        def first(i, x):
            r = win(i * TILE)
            do[r, :] = dot(dr[r, :].astype(bf16), wout[...], NT).astype(bf16)
            return x

        lax.fori_loop(0, n, first, 0)
        attend_back(counts, qkv, do, lse, dqkv, samples, width)
        dqkv[win(total), :] = jnp.zeros((TILE, dqkv.shape[1]), bf16)

    return body


def proj_other_body(samples, patches):
    def body(counts, line, dr, dqkv, wqkv, da, h, gain, out, g1, dh):
        n = tiles(total_of(counts, samples))
        g1[...] = jnp.zeros(g1.shape, f32)

        def last(i, x):
            r = win(i * TILE)
            dat = da[r, :] + dot(dqkv[r, :], wqkv[...], NT)
            hat, inv = normed(h[r, :].astype(f32))
            g1[0:1, :] += jnp.sum(dat * hat, axis=0, keepdims=True)
            g1[1:2, :] += jnp.sum(dat, axis=0, keepdims=True)
            dh[r, :] = (dr[r, :] + norm_back(dat, hat, inv, gain[...])).astype(bf16)
            return x

        lax.fori_loop(0, n, last, 0)
        dh[win(n * TILE), :] = jnp.zeros((TILE, dh.shape[1]), bf16)

        def scatter(s, start):
            out[s] = dot(hot_back(counts, line, s, patches), dh[win(start), :]).astype(bf16)
            return start + ((counts[s] + 15) // 16) * 16

        lax.fori_loop(0, samples, scatter, 0)

    return body


def sds(shape, dtype):
    return jax.ShapeDtypeStruct(shape, dtype)


def call(body, counts, args, outs, scratch=(), flops=0):
    moved = sum(x.size * x.dtype.itemsize for x in list(args) + list(outs))
    return pl.pallas_call(
        body,
        out_shape=list(outs),
        grid_spec=pltpu.PrefetchScalarGridSpec(
            num_scalar_prefetch=1,
            grid=(1,),
            in_specs=[pl.BlockSpec(x.shape, lambda i, n, d=x.ndim: (0,) * d, pipeline_mode=pl.Buffered(1)) for x in args],
            out_specs=[pl.BlockSpec(x.shape, lambda i, n, d=len(x.shape): (0,) * d, pipeline_mode=pl.Buffered(1)) for x in outs],
            scratch_shapes=list(scratch),
        ),
        compiler_params=pltpu.CompilerParams(vmem_limit_bytes=62 << 20),
        cost_estimate=pl.CostEstimate(flops=flops, transcendentals=0, bytes_accessed=moved),
    )(counts, *args)


def fwd_own(counts, col, patches, cot, gain, shift, weight):
    S, L, D = patches.shape
    width = weight.shape[1] // 3
    TP = S * SLOTS + TILE
    whole = lambda d: (lambda s, n: (0,) * d)
    one = lambda s, n: (s, 0, 0)
    B1 = pl.Buffered(1)
    outs = [sds((TP, D), bf16), sds((TP, D), bf16), sds((TP, D), bf16), sds((TP, 3 * width), bf16), sds((TP, width), bf16), sds((S, width // 128, 2, SLOTS), f32)]
    return pl.pallas_call(
        fwd_own_body(S, width),
        name="fwd_own",
        out_shape=outs,
        grid_spec=pltpu.PrefetchScalarGridSpec(
            num_scalar_prefetch=1,
            grid=(S,),
            in_specs=[
                pl.BlockSpec((1, L, 1), one),
                pl.BlockSpec((1, L, D), one),
                pl.BlockSpec((1, L, D), one),
                pl.BlockSpec((1, D), whole(2)),
                pl.BlockSpec((1, D), whole(2)),
                pl.BlockSpec(weight.shape, whole(2), pipeline_mode=B1),
            ],
            out_specs=[pl.BlockSpec(x.shape, whole(len(x.shape)), pipeline_mode=B1) for x in outs],
        ),
        compiler_params=pltpu.CompilerParams(vmem_limit_bytes=62 << 20),
        cost_estimate=pl.CostEstimate(flops=6 * 10**9, transcendentals=0, bytes_accessed=25 << 20),
    )(counts, col, patches, cot, gain, shift, weight)


def fwd_other(counts, a, h, o, wq, out_own, wo, gain, shift, S):
    TP, D = a.shape
    width = wq[0].shape[1] // 3
    outs = [sds((TP, 3 * width), bf16), sds((TP, width), bf16), sds((S, width // 128, 2, SLOTS), f32), sds((TP, D), f32), sds((TP, D), bf16), sds((D, 3 * width), bf16), sds((width, D), bf16)]
    return call(fwd_other_body(S, width), counts, [a, h, o, *wq, *wo, out_own, gain, shift], outs, flops=7 * 10**9)


def mlp_own(counts, c, dm, up, down, S):
    TP, D = c.shape
    outs = [sds((TP, D), f32), sds((TP, D), f32), sds(up.shape, f32), sds(down.shape, f32)]
    return call(mlp_own_body(S), counts, [c, dm, up, down], outs, flops=18 * 10**9)


def mlp_other(counts, line, c, dm, up, down, m, dc, r, gain, S, L):
    TP, D = c.shape
    outs = [sds((S, L, D), bf16), sds((TP, D), f32), sds((8, D), f32)]
    return call(mlp_other_body(S, L), counts, [line, c, dm, *up, *down, m, dc, r, gain], outs, [pltpu.VMEM((TP, D), bf16), pltpu.VMEM((D, 4 * down[0].shape[0]), bf16), pltpu.VMEM((4 * down[0].shape[0], D), bf16)], flops=12 * 10**9)


def attn_own(counts, dr, qkv, lse, o, wout, S):
    TP, width = o.shape
    outs = [sds(wout.shape, f32), sds((TP, 3 * width), bf16)]
    return call(attn_own_body(S, width), counts, [dr, qkv, lse, o, wout], outs, [pltpu.VMEM((TP, width), bf16)], flops=5 * 10**9)


def proj_own(counts, dqkv, a, wqkv, S):
    TP, D = a.shape
    width = wqkv.shape[1] // 3
    outs = [sds((TP, D), f32), sds((3, D, width), f32)]
    return call(proj_own_body(S, width), counts, [dqkv, a, wqkv], outs, flops=5 * 10**9)


def attn_other(counts, dr, qkv, lse, wout, S):
    TP, width = dr.shape[0], wout.shape[0]
    outs = [sds((TP, 3 * width), bf16)]
    return call(attn_other_body(S, width), counts, [dr, qkv, lse, wout], outs, [pltpu.VMEM((TP, width), bf16)], flops=4 * 10**9)[0]


def proj_other(counts, line, dr, dqkv, wqkv, da, h, gain, S, L):
    TP, D = h.shape
    outs = [sds((S, L, D), bf16), sds((8, D), f32)]
    return call(proj_other_body(S, L), counts, [line, dr, dqkv, wqkv, da, h, gain], outs, [pltpu.VMEM((TP, D), bf16)], flops=4 * 10**9)


def swap(x, axis, size, bit):
    return lax.ppermute(x, axis, [(k, k ^ bit) for k in range(size)])


def tie(*xs):
    return lax.optimization_barrier(xs)


def side(bit):
    return (lax.axis_index("dp") // bit) % 2


def half(x, i):
    n = x.shape[0] // 2
    return lax.dynamic_slice_in_dim(x, i * n, n, 0)


def fold(x, bit, dp):
    i = side(bit)
    return half(x, i) + swap(half(x, 1 - i), "dp", dp, bit)


def spread(x, bit, dp):
    got = swap(x, "dp", dp, bit)
    first = side(bit) == 0
    return jnp.where(first, jnp.concatenate([x, got], 0), jnp.concatenate([got, x], 0))


def folds(x, bits, dp):
    for bit in bits:
        x = fold(x, bit, dp)
    return x


def spreads(x, bits, dp):
    for bit in reversed(bits):
        x = spread(x, bit, dp)
    return x


def shards(dp, patches, counts, visible, g1, b1, wq, wo, g2, b2, wu, wd, cot):
    S, L, D = patches.shape
    wt = wq.transpose(1, 0, 2)
    wq = jnp.concatenate([wt[0], wt[1], wt[2]], axis=1)
    col, line = visible[:, :, None], visible[:, None, :]
    g1, b1, g2, b2 = (x[None, :] for x in (g1, b1, g2, b2))
    me = lax.axis_index("dp") % 4
    order = jnp.stack([me, me ^ 2, me ^ 1, me ^ 3]).astype(jnp.int32)

    def part(w):
        rows = w.shape[0] // 4
        return lax.dynamic_slice_in_dim(w, me * rows, rows, 0).astype(f32)

    def rest(first, across):
        return [first, across, swap(first, "dp", dp, 1), swap(across, "dp", dp, 1)]

    counts = jnp.concatenate([counts, order])
    every = [1 << i for i in range(dp.bit_length() - 1)]
    along = every
    other = [1, 4, 2] + every[3:] if len(every) > 2 else every

    fq, fo = swap(part(wq), "tensor", 2, 1), swap(part(wo), "tensor", 2, 1)
    h, dm, a, qkv0, o0, lse0 = fwd_own(counts, col, patches, cot, g1, b1, wq)
    fq, fo, pu, pd, a = tie(fq, fo, part(wu), part(wd), a)
    aq = swap(fq, "dp", dp, 2)
    ao = swap(fo, "dp", dp, 2)
    fu = swap(pu, "tensor", 2, 1)
    fd = swap(pd, "tensor", 2, 1)
    wq1, wo1 = rest(fq, aq), rest(fo, ao)
    qkv1, _, lse1, r, c, wq1, wo1 = fwd_other(counts, a, h, o0, wq1, wo, wo1, g2, b2, S)
    fu, fd, c = tie(fu, fd, c)
    au = swap(fu, "dp", dp, 2)
    ad = swap(fd, "dp", dp, 2)
    m, dc, gup, gdown = mlp_own(counts, c, dm, wu, wd, S)
    au, ad, m = tie(au, ad, m)
    wu1, wd1 = rest(fu, au), rest(fd, ad)
    A, B = fold(gup, 1, dp), fold(gdown, 1, dp)
    A, B, c = tie(A, B, c)
    out, dr, gg2 = mlp_other(counts, line, c, dm, wu1, wd1, m, dc, r, g2, S, L)
    A, B = fold(A, along[1], dp), fold(B, other[1], dp)
    A, B, dr = tie(A, B, dr)
    A, B = fold(A, along[2], dp), fold(B, other[2], dp)
    gout, dq0 = attn_own(counts, dr, qkv0, lse0, o0, wo, S)
    A, B, dq0, dr = tie(A, B, dq0, dr)
    A, B, E = folds(A, along[3:], dp), folds(B, other[3:], dp), fold(gout, 1, dp)
    da, gqkv = proj_own(counts, dq0, a, wq, S)
    C = gqkv.reshape(2, (3 * D) // 2, -1)
    C, F = fold(C[0], 1, dp), fold(C[1], 1, dp)
    da, dr = tie(da, dr)
    dq1 = attn_other(counts, dr, qkv1, lse1, wo1, S)
    A, B, C, F, E, dq1 = tie(A, B, C, F, E, dq1)
    A, B = spreads(A, along[3:], dp), spreads(B, other[3:], dp)
    C, F, E = fold(C, along[1], dp), fold(F, other[1], dp), fold(E, other[1], dp)
    gin, gg1 = proj_other(counts, line, dr, dq1, wq1, da, h, g1, S, L)
    C, F, E, A, B, gg1 = tie(C, F, E, A, B, gg1)
    small = jnp.concatenate([gg1, gg2], 0)
    for bit in along[3:]:
        small = small + swap(small, "dp", dp, bit)
    for bit, late in zip(reversed(along[:3]), reversed(other[:3])):
        A, B = spread(A, bit, dp), spread(B, late, dp)
        small = small + swap(small, "dp", dp, bit)
        if bit != 1:
            A, B, small = tie(A, B, small)
    gup, gdown = A, B
    gg1, gg2 = small[:8], small[8:]
    C = spreads(folds(C, along[2:], dp), along, dp)
    F = spreads(folds(F, other[2:], dp), other, dp)
    gqkv = jnp.concatenate([C, F], 0).reshape(3, D, -1)
    gout = spreads(folds(E, other[2:], dp), other, dp)
    return (out, gin, gg1[0], gg1[1], gqkv.transpose(1, 0, 2), gout, gg2[0], gg2[1], gup, gdown)


def solution(mesh):
    dp = mesh.shape["dp"]
    placed = (P("dp", None, None), P("dp"), P("dp", None), P(), P(), P(None, None, "tensor"), P("tensor", None), P(), P(), P(None, "tensor"), P("tensor", None), P("dp", None, None))
    outs = (P("dp", None, None), P("dp", None, None), P(), P(), P(None, None, "tensor"), P("tensor", None), P(), P(), P(None, "tensor"), P("tensor", None))

    def layer(*a):
        return shards(dp, *a)

    return jax.shard_map(layer, mesh=mesh, in_specs=placed, out_specs=outs, check_vma=False)
```

```python
import jax
import jax.numpy as jnp
from jax import lax
from jax.sharding import PartitionSpec as P
from jax.experimental import pallas as pl
from jax.experimental.pallas import tpu as pltpu

HD = 64
SLOTS = 256
TILE = 256
norm_eps = 1e-06
masked_score = -1e30
scale = HD ** (-0.5)
f32, bf16 = jnp.float32, jnp.bfloat16


def dot(x, y, dims=((1,), (0,))):
    return lax.dot_general(x, y, (dims, ((), ())), preferred_element_type=f32)


NT = ((1,), (1,))
TN = ((0,), (0,))


def win(start, size=SLOTS):
    if not isinstance(start, int):
        start = pl.multiple_of(start, 16)
    return pl.ds(start, size)


def start_of(counts, s):
    return lax.fori_loop(0, s, lambda i, t: t + ((counts[i] + 15) // 16) * 16, 0)


def total_of(counts, samples):
    return start_of(counts, samples)


def normed(values):
    center = values - jnp.mean(values, axis=-1, keepdims=True)
    spread = jnp.mean(center * center, axis=-1, keepdims=True)
    inv = lax.rsqrt(spread + norm_eps)
    return center * inv, inv


def norm_back(grad, hat, inv, gain):
    g = grad * gain
    return inv * (g - jnp.mean(g, axis=-1, keepdims=True) - hat * jnp.mean(g * hat, axis=-1, keepdims=True))


def lane_halves():
    lane = lax.broadcasted_iota(jnp.int32, (1, 128), 1)
    return lane < HD


def by_size(counts, s, run):
    few = counts[s] <= SLOTS // 2

    @pl.when(few)
    def _():
        run(SLOTS // 2)

    @pl.when(jnp.logical_not(few))
    def _():
        run(SLOTS)


def lanes(start):
    return slice(start, start + 128)


def attend_rows(counts, qkv, out, lse, samples, width):
    left = lane_halves()

    def one(s, start):
        def run(size):
            rows = win(start, size)
            live = lax.broadcasted_iota(jnp.int32, (size, 1), 0) < counts[s]

            def pair(j, x):
                lo = j * 128
                q = qkv[rows, lanes(lo)]
                k = qkv[rows, lanes(width + lo)]
                v = qkv[rows, lanes(2 * width + lo)]
                parts = []
                for side in range(2):
                    keep = left if side == 0 else ~left
                    sc = dot(jnp.where(keep, k, jnp.zeros_like(k)), q, NT) * scale
                    sc = jnp.where(live, sc, masked_score)
                    top = jnp.max(sc, axis=0, keepdims=True)
                    w = jnp.exp(sc - top)
                    tot = jnp.sum(w, axis=0, keepdims=True)
                    lse[s, j, side:side + 1, :size] = top + jnp.log(tot)
                    if size < SLOTS:
                        lse[s, j, side:side + 1, size:] = jnp.full((1, SLOTS - size), 1e30, f32)
                    p = (w * (1.0 / tot)).astype(bf16)
                    parts.append(dot(p, v, TN))
                out[rows, lanes(lo)] = jnp.where(left, parts[0], parts[1]).astype(bf16)
                return x

            for j in range(width // 128):
                pair(j, 0)

        by_size(counts, s, run)
        return start + ((counts[s] + 15) // 16) * 16

    lax.fori_loop(0, samples, one, 0)


def tiles(total):
    return (total + TILE - 1) // TILE


def fwd_own_body(samples, width):
    def body(counts, col, patches, cot, gain, shift, weight, h, dm, a, qkv, o, lse):
        s = pl.program_id(0)
        start = start_of(counts, s)
        pick = col[0, :SLOTS, :]
        row = lax.broadcasted_iota(jnp.int32, (SLOTS, 1), 0)
        pick = jnp.where(row < counts[s], pick, -1)
        hot = (lax.broadcasted_iota(jnp.int32, (SLOTS, patches.shape[1]), 1) == pick).astype(f32).astype(bf16)
        h[win(start), :] = dot(hot, patches[0]).astype(bf16)
        dm[win(start), :] = dot(hot, cot[0]).astype(bf16)

        @pl.when(s == samples - 1)
        def _():
            total = total_of(counts, samples)
            zeros = jnp.zeros((TILE, h.shape[1]), bf16)
            h[win(total), :] = zeros
            dm[win(total), :] = zeros

            def tile(i, c):
                r = win(i * TILE)
                hat, _ = normed(h[r, :].astype(f32))
                av = (hat * gain[...] + shift[...]).astype(bf16)
                a[r, :] = av
                qkv[r, :] = dot(av, weight[...]).astype(bf16)
                return c

            n = tiles(total)
            lax.fori_loop(0, n, tile, 0)
            qkv[win(n * TILE), :] = jnp.zeros((TILE, qkv.shape[1]), bf16)
            attend_rows(counts, qkv, o, lse, samples, width)
            o[win(total), :] = jnp.zeros((TILE, width), bf16)

    return body


def join(counts, samples, pieces, full):
    rows = pieces[0].shape[0]
    for i in range(4):
        full[pl.ds(pl.multiple_of(counts[samples + i] * rows, 16), rows), :] = pieces[i][...].astype(bf16)


def fwd_other_body(samples, width):
    def body(counts, a, h, o, q0, q1, q2, q3, w0, w1, w2, w3, out_own, gain, shift, qkv, o2, lse, r, c, weight, out_other):
        join(counts, samples, (q0, q1, q2, q3), weight)
        join(counts, samples, (w0, w1, w2, w3), out_other)
        total = total_of(counts, samples)
        n = tiles(total)

        def tile(i, x):
            rr = win(i * TILE)
            qkv[rr, :] = dot(a[rr, :], weight[...]).astype(bf16)
            return x

        lax.fori_loop(0, n, tile, 0)
        qkv[win(n * TILE), :] = jnp.zeros((TILE, qkv.shape[1]), bf16)
        attend_rows(counts, qkv, o2, lse, samples, width)
        o2[win(total), :] = jnp.zeros((TILE, width), bf16)

        def tail(i, x):
            rr = win(i * TILE)
            z = dot(o[rr, :], out_own[...]) + dot(o2[rr, :], out_other[...])
            rv = h[rr, :].astype(f32) + z
            r[rr, :] = rv
            hat, _ = normed(rv)
            c[rr, :] = (hat * gain[...] + shift[...]).astype(bf16)
            return x

        lax.fori_loop(0, n, tail, 0)

    return body


def gelu_both(u):
    cdf = 0.5 * (1.0 + lax.erf(u * (0.5 ** 0.5)))
    pdf = jnp.exp(-0.5 * u * u) * (0.5 / jnp.pi) ** 0.5
    return u * cdf, cdf + u * pdf


def mlp_tile(cv, dv, up, down):
    u = dot(cv, up[...])
    e, slope = gelu_both(u)
    e = e.astype(bf16)
    m = dot(e, down[...])
    de = dot(dv, down[...], NT)
    du = (de * slope).astype(bf16)
    dc = dot(du, up[...], NT)
    return e, du, m, dc


def mlp_own_body(samples):
    def body(counts, c, dm, up, down, m, dc, gup, gdown):
        n = tiles(total_of(counts, samples))
        gup[...] = jnp.zeros(gup.shape, f32)
        gdown[...] = jnp.zeros(gdown.shape, f32)

        def tile(i, x):
            r = win(i * TILE)
            cv, dv = c[r, :], dm[r, :]
            e, du, mv, dcv = mlp_tile(cv, dv, up, down)
            m[r, :] = mv
            dc[r, :] = dcv
            gdown[...] += dot(e, dv, TN)
            gup[...] += dot(cv, du, TN)
            return x

        lax.fori_loop(0, n, tile, 0)

    return body


def hot_back(counts, line, s, patches):
    live = lax.broadcasted_iota(jnp.int32, (1, SLOTS), 1) < counts[s]
    pick = jnp.where(live, line[s, :, :SLOTS], -1)
    return (lax.broadcasted_iota(jnp.int32, (patches, SLOTS), 0) == pick).astype(f32).astype(bf16)


def mlp_other_body(samples, patches):
    def body(counts, line, c, dm, u0, u1, u2, u3, d0, d1, d2, d3, m, dc, r, gain, out, dr, g2, y, up, down):
        join(counts, samples, (u0, u1, u2, u3), up)
        join(counts, samples, (d0, d1, d2, d3), down)
        n = tiles(total_of(counts, samples))
        g2[...] = jnp.zeros(g2.shape, f32)

        def tile(i, x):
            rr = win(i * TILE)
            cv, dv = c[rr, :], dm[rr, :]
            _, _, mv, dcv = mlp_tile(cv, dv, up, down)
            rv = r[rr, :]
            y[rr, :] = (rv + (m[rr, :] + mv)).astype(bf16)
            dct = dc[rr, :] + dcv
            hat, inv = normed(rv)
            g2[0:1, :] += jnp.sum(dct * hat, axis=0, keepdims=True)
            g2[1:2, :] += jnp.sum(dct, axis=0, keepdims=True)
            dr[rr, :] = dv.astype(f32) + norm_back(dct, hat, inv, gain[...])
            return x

        lax.fori_loop(0, n, tile, 0)
        y[win(n * TILE), :] = jnp.zeros((TILE, y.shape[1]), bf16)

        def scatter(s, start):
            out[s] = dot(hot_back(counts, line, s, patches), y[win(start), :]).astype(bf16)
            return start + ((counts[s] + 15) // 16) * 16

        lax.fori_loop(0, samples, scatter, 0)

    return body


def attend_back(counts, qkv, do, lse, dqkv, samples, width):
    left = lane_halves()

    def one(s, start):
        def run(size):
            rows = win(start, size)
            live = lax.broadcasted_iota(jnp.int32, (size, 1), 0) < counts[s]

            def pair(j, x):
                lo = j * 128
                q = qkv[rows, lanes(lo)]
                k = qkv[rows, lanes(width + lo)]
                v = qkv[rows, lanes(2 * width + lo)]
                dov = do[rows, lanes(lo)]
                dov = jnp.where(live, dov, jnp.zeros_like(dov))
                zero = jnp.zeros_like(k)
                dq, dk, dvv = [], [], []
                for side in range(2):
                    keep = left if side == 0 else ~left
                    sc = dot(jnp.where(keep, k, zero), q, NT) * scale
                    sc = jnp.where(live, sc, masked_score)
                    p = jnp.exp(sc - lse[s, j, side:side + 1, :size])
                    dp = dot(jnp.where(keep, v, zero), dov, NT)
                    t = jnp.sum(p * dp, axis=0, keepdims=True)
                    ds = (p * (dp - t)).astype(bf16)
                    dq.append(dot(ds, k, TN))
                    dk.append(dot(ds, q))
                    dvv.append(dot(p.astype(bf16), dov))
                dqkv[rows, lanes(lo)] = (jnp.where(left, dq[0], dq[1]) * scale).astype(bf16)
                dqkv[rows, lanes(width + lo)] = (jnp.where(left, dk[0], dk[1]) * scale).astype(bf16)
                dqkv[rows, lanes(2 * width + lo)] = jnp.where(left, dvv[0], dvv[1]).astype(bf16)
                return x

            for j in range(width // 128):
                pair(j, 0)

        run(SLOTS)
        return start + ((counts[s] + 15) // 16) * 16

    lax.fori_loop(0, samples, one, 0)


def attn_own_body(samples, width):
    def body(counts, dr, qkv, lse, o, wout, gout, dqkv, do):
        total = total_of(counts, samples)
        n = tiles(total)
        gout[...] = jnp.zeros(gout.shape, f32)

        def first(i, x):
            r = win(i * TILE)
            dz = dr[r, :].astype(bf16)
            do[r, :] = dot(dz, wout[...], NT).astype(bf16)
            gout[...] += dot(o[r, :], dz, TN)
            return x

        lax.fori_loop(0, n, first, 0)
        attend_back(counts, qkv, do, lse, dqkv, samples, width)
        dqkv[win(total), :] = jnp.zeros((TILE, dqkv.shape[1]), bf16)

    return body


def proj_own_body(samples, width):
    def body(counts, dqkv, a, wqkv, da, gqkv):
        n = tiles(total_of(counts, samples))
        gqkv[...] = jnp.zeros(gqkv.shape, f32)

        def last(i, x):
            r = win(i * TILE)
            dv = dqkv[r, :]
            da[r, :] = dot(dv, wqkv[...], NT)
            for j in range(3):
                gqkv[j] += dot(a[r, :], dv[:, j * width:(j + 1) * width], TN)
            return x

        lax.fori_loop(0, n, last, 0)

    return body


def attn_other_body(samples, width):
    def body(counts, dr, qkv, lse, wout, dqkv, do):
        total = total_of(counts, samples)
        n = tiles(total)

        def first(i, x):
            r = win(i * TILE)
            do[r, :] = dot(dr[r, :].astype(bf16), wout[...], NT).astype(bf16)
            return x

        lax.fori_loop(0, n, first, 0)
        attend_back(counts, qkv, do, lse, dqkv, samples, width)
        dqkv[win(total), :] = jnp.zeros((TILE, dqkv.shape[1]), bf16)

    return body


def proj_other_body(samples, patches):
    def body(counts, line, dr, dqkv, wqkv, da, h, gain, out, g1, dh):
        n = tiles(total_of(counts, samples))
        g1[...] = jnp.zeros(g1.shape, f32)

        def last(i, x):
            r = win(i * TILE)
            dat = da[r, :] + dot(dqkv[r, :], wqkv[...], NT)
            hat, inv = normed(h[r, :].astype(f32))
            g1[0:1, :] += jnp.sum(dat * hat, axis=0, keepdims=True)
            g1[1:2, :] += jnp.sum(dat, axis=0, keepdims=True)
            dh[r, :] = (dr[r, :] + norm_back(dat, hat, inv, gain[...])).astype(bf16)
            return x

        lax.fori_loop(0, n, last, 0)
        dh[win(n * TILE), :] = jnp.zeros((TILE, dh.shape[1]), bf16)

        def scatter(s, start):
            out[s] = dot(hot_back(counts, line, s, patches), dh[win(start), :]).astype(bf16)
            return start + ((counts[s] + 15) // 16) * 16

        lax.fori_loop(0, samples, scatter, 0)

    return body


def sds(shape, dtype):
    return jax.ShapeDtypeStruct(shape, dtype)


def call(body, counts, args, outs, scratch=(), flops=0):
    moved = sum(x.size * x.dtype.itemsize for x in list(args) + list(outs))
    return pl.pallas_call(
        body,
        out_shape=list(outs),
        grid_spec=pltpu.PrefetchScalarGridSpec(
            num_scalar_prefetch=1,
            grid=(1,),
            in_specs=[pl.BlockSpec(x.shape, lambda i, n, d=x.ndim: (0,) * d, pipeline_mode=pl.Buffered(1)) for x in args],
            out_specs=[pl.BlockSpec(x.shape, lambda i, n, d=len(x.shape): (0,) * d, pipeline_mode=pl.Buffered(1)) for x in outs],
            scratch_shapes=list(scratch),
        ),
        compiler_params=pltpu.CompilerParams(vmem_limit_bytes=62 << 20),
        cost_estimate=pl.CostEstimate(flops=flops, transcendentals=0, bytes_accessed=moved),
    )(counts, *args)


def fwd_own(counts, col, patches, cot, gain, shift, weight):
    S, L, D = patches.shape
    width = weight.shape[1] // 3
    TP = S * SLOTS + TILE
    whole = lambda d: (lambda s, n: (0,) * d)
    one = lambda s, n: (s, 0, 0)
    B1 = pl.Buffered(1)
    outs = [sds((TP, D), bf16), sds((TP, D), bf16), sds((TP, D), bf16), sds((TP, 3 * width), bf16), sds((TP, width), bf16), sds((S, width // 128, 2, SLOTS), f32)]
    return pl.pallas_call(
        fwd_own_body(S, width),
        name="fwd_own",
        out_shape=outs,
        grid_spec=pltpu.PrefetchScalarGridSpec(
            num_scalar_prefetch=1,
            grid=(S,),
            in_specs=[
                pl.BlockSpec((1, L, 1), one),
                pl.BlockSpec((1, L, D), one),
                pl.BlockSpec((1, L, D), one),
                pl.BlockSpec((1, D), whole(2)),
                pl.BlockSpec((1, D), whole(2)),
                pl.BlockSpec(weight.shape, whole(2), pipeline_mode=B1),
            ],
            out_specs=[pl.BlockSpec(x.shape, whole(len(x.shape)), pipeline_mode=B1) for x in outs],
        ),
        compiler_params=pltpu.CompilerParams(vmem_limit_bytes=62 << 20),
        cost_estimate=pl.CostEstimate(flops=6 * 10**9, transcendentals=0, bytes_accessed=25 << 20),
    )(counts, col, patches, cot, gain, shift, weight)


def fwd_other(counts, a, h, o, wq, out_own, wo, gain, shift, S):
    TP, D = a.shape
    width = wq[0].shape[1] // 3
    outs = [sds((TP, 3 * width), bf16), sds((TP, width), bf16), sds((S, width // 128, 2, SLOTS), f32), sds((TP, D), f32), sds((TP, D), bf16), sds((D, 3 * width), bf16), sds((width, D), bf16)]
    return call(fwd_other_body(S, width), counts, [a, h, o, *wq, *wo, out_own, gain, shift], outs, flops=7 * 10**9)


def mlp_own(counts, c, dm, up, down, S):
    TP, D = c.shape
    outs = [sds((TP, D), f32), sds((TP, D), f32), sds(up.shape, f32), sds(down.shape, f32)]
    return call(mlp_own_body(S), counts, [c, dm, up, down], outs, flops=18 * 10**9)


def mlp_other(counts, line, c, dm, up, down, m, dc, r, gain, S, L):
    TP, D = c.shape
    outs = [sds((S, L, D), bf16), sds((TP, D), f32), sds((8, D), f32)]
    return call(mlp_other_body(S, L), counts, [line, c, dm, *up, *down, m, dc, r, gain], outs, [pltpu.VMEM((TP, D), bf16), pltpu.VMEM((D, 4 * down[0].shape[0]), bf16), pltpu.VMEM((4 * down[0].shape[0], D), bf16)], flops=12 * 10**9)


def attn_own(counts, dr, qkv, lse, o, wout, S):
    TP, width = o.shape
    outs = [sds(wout.shape, f32), sds((TP, 3 * width), bf16)]
    return call(attn_own_body(S, width), counts, [dr, qkv, lse, o, wout], outs, [pltpu.VMEM((TP, width), bf16)], flops=5 * 10**9)


def proj_own(counts, dqkv, a, wqkv, S):
    TP, D = a.shape
    width = wqkv.shape[1] // 3
    outs = [sds((TP, D), f32), sds((3, D, width), f32)]
    return call(proj_own_body(S, width), counts, [dqkv, a, wqkv], outs, flops=5 * 10**9)


def attn_other(counts, dr, qkv, lse, wout, S):
    TP, width = dr.shape[0], wout.shape[0]
    outs = [sds((TP, 3 * width), bf16)]
    return call(attn_other_body(S, width), counts, [dr, qkv, lse, wout], outs, [pltpu.VMEM((TP, width), bf16)], flops=4 * 10**9)[0]


def proj_other(counts, line, dr, dqkv, wqkv, da, h, gain, S, L):
    TP, D = h.shape
    outs = [sds((S, L, D), bf16), sds((8, D), f32)]
    return call(proj_other_body(S, L), counts, [line, dr, dqkv, wqkv, da, h, gain], outs, [pltpu.VMEM((TP, D), bf16)], flops=4 * 10**9)


def swap(x, axis, size, bit):
    return lax.ppermute(x, axis, [(k, k ^ bit) for k in range(size)])


def tie(*xs):
    return lax.optimization_barrier(xs)


def side(bit):
    return (lax.axis_index("dp") // bit) % 2


def half(x, i):
    n = x.shape[0] // 2
    return lax.dynamic_slice_in_dim(x, i * n, n, 0)


def fold(x, bit, dp):
    i = side(bit)
    return half(x, i) + swap(half(x, 1 - i), "dp", dp, bit)


def spread(x, bit, dp):
    got = swap(x, "dp", dp, bit)
    first = side(bit) == 0
    return jnp.where(first, jnp.concatenate([x, got], 0), jnp.concatenate([got, x], 0))


def folds(x, bits, dp):
    for bit in bits:
        x = fold(x, bit, dp)
    return x


def spreads(x, bits, dp):
    for bit in reversed(bits):
        x = spread(x, bit, dp)
    return x


def shards(dp, patches, counts, visible, g1, b1, wq, wo, g2, b2, wu, wd, cot):
    S, L, D = patches.shape
    wt = wq.transpose(1, 0, 2)
    wq = jnp.concatenate([wt[0], wt[1], wt[2]], axis=1)
    col, line = visible[:, :, None], visible[:, None, :]
    g1, b1, g2, b2 = (x[None, :] for x in (g1, b1, g2, b2))
    me = lax.axis_index("dp") % 4
    order = jnp.stack([me, me ^ 2, me ^ 1, me ^ 3]).astype(jnp.int32)

    def part(w):
        rows = w.shape[0] // 4
        return lax.dynamic_slice_in_dim(w, me * rows, rows, 0).astype(f32)

    def rest(first, across):
        return [first, across, swap(first, "dp", dp, 1), swap(across, "dp", dp, 1)]

    counts = jnp.concatenate([counts, order])
    every = [1 << i for i in range(dp.bit_length() - 1)]
    along = every
    other = [1, 4, 2] + every[3:] if len(every) > 2 else every

    fq, fo = swap(part(wq), "tensor", 2, 1), swap(part(wo), "tensor", 2, 1)
    h, dm, a, qkv0, o0, lse0 = fwd_own(counts, col, patches, cot, g1, b1, wq)
    fq, fo, pu, pd, a = tie(fq, fo, part(wu), part(wd), a)
    aq = swap(fq, "dp", dp, 2)
    ao = swap(fo, "dp", dp, 2)
    fu = swap(pu, "tensor", 2, 1)
    fd = swap(pd, "tensor", 2, 1)
    wq1, wo1 = rest(fq, aq), rest(fo, ao)
    qkv1, _, lse1, r, c, wq1, wo1 = fwd_other(counts, a, h, o0, wq1, wo, wo1, g2, b2, S)
    fu, fd, c = tie(fu, fd, c)
    au = swap(fu, "dp", dp, 2)
    ad = swap(fd, "dp", dp, 2)
    m, dc, gup, gdown = mlp_own(counts, c, dm, wu, wd, S)
    au, ad, m = tie(au, ad, m)
    wu1, wd1 = rest(fu, au), rest(fd, ad)
    A, B = fold(gup, 1, dp), fold(gdown, 1, dp)
    A, B, c = tie(A, B, c)
    out, dr, gg2 = mlp_other(counts, line, c, dm, wu1, wd1, m, dc, r, g2, S, L)
    A, B = fold(A, along[1], dp), fold(B, other[1], dp)
    A, B, dr = tie(A, B, dr)
    A, B = fold(A, along[2], dp), fold(B, other[2], dp)
    gout, dq0 = attn_own(counts, dr, qkv0, lse0, o0, wo, S)
    A, B, dq0, dr = tie(A, B, dq0, dr)
    A, B = folds(A, along[3:], dp), folds(B, other[3:], dp)
    da, gqkv = proj_own(counts, dq0, a, wq, S)
    width = gout.shape[0]
    flat = [gqkv.reshape(3 * D, width)] + [gout[:, j:j + width] for j in range(0, D, width)]
    C = jnp.concatenate(flat, 0).reshape(2, -1, width)
    C, F = fold(C[0], 1, dp), fold(C[1], 1, dp)
    da, dr = tie(da, dr)
    dq1 = attn_other(counts, dr, qkv1, lse1, wo1, S)
    A, B, C, F, dq1 = tie(A, B, C, F, dq1)
    A, B = spreads(A, along[3:], dp), spreads(B, other[3:], dp)
    C, F = fold(C, along[1], dp), fold(F, other[1], dp)
    gin, gg1 = proj_other(counts, line, dr, dq1, wq1, da, h, g1, S, L)
    C, F, A, B, gg1 = tie(C, F, A, B, gg1)
    small = jnp.concatenate([gg1, gg2], 0)
    for bit in along[3:]:
        small = small + swap(small, "dp", dp, bit)
    for bit, late in zip(reversed(along[:3]), reversed(other[:3])):
        A, B = spread(A, bit, dp), spread(B, late, dp)
        small = small + swap(small, "dp", dp, bit)
        if bit != 1:
            A, B, small = tie(A, B, small)
    gup, gdown = A, B
    gg1, gg2 = small[:8], small[8:]
    C = spreads(folds(C, along[2:], dp), along, dp)
    F = spreads(folds(F, other[2:], dp), other, dp)
    flat = jnp.concatenate([C, F], 0)
    gqkv = flat[:3 * D].reshape(3, D, width)
    gout = jnp.concatenate([flat[j:j + width] for j in range(3 * D, 4 * D, width)], 1)
    return (out, gin, gg1[0], gg1[1], gqkv.transpose(1, 0, 2), gout, gg2[0], gg2[1], gup, gdown)


def solution(mesh):
    dp = mesh.shape["dp"]
    placed = (P("dp", None, None), P("dp"), P("dp", None), P(), P(), P(None, None, "tensor"), P("tensor", None), P(), P(), P(None, "tensor"), P("tensor", None), P("dp", None, None))
    outs = (P("dp", None, None), P("dp", None, None), P(), P(), P(None, None, "tensor"), P("tensor", None), P(), P(), P(None, "tensor"), P("tensor", None))

    def layer(*a):
        return shards(dp, *a)

    return jax.shard_map(layer, mesh=mesh, in_specs=placed, out_specs=outs, check_vma=False)
```
